1024 devices in a mesh: sa: 32 (over y, x), gx: 8 (over z_lo, core), gy: 4 (over z_hi).
Axes of the slice: x: 4, y: 8, z: 16 (z_hi: 4, z_lo: 4; z = z_hi * 4 + z_lo), core: 2. Of those that a mesh axis runs over, the one named last changes fastest.
Arguments:
- vectors: float32 [32, 16, 8, 24, 256], P('sa', 'gx', 'gy'), may hold values from -6 to 6
- gauge_links: float32 [16, 8, 72, 256], P('gx', 'gy'), may hold values from -1 to 1, as said below
Outputs:
- filtered_once: float32 [32, 16, 8, 24, 256], P('sa', 'gx', 'gy')
- filtered_twice: float32 [32, 16, 8, 24, 256], P('sa', 'gx', 'gy')
The draws below stay inside these ranges and needn't reach their ends.
Inputs may be any that keep to these rules, and one draw needn't show every extreme that they name: `gauge_links`: for each site and direction the nine complex entries form a special unitary 3 x 3 matrix.
All inputs are finite; a program needn't handle non-finite values.
Results may differ from the reference program's by a relative error of at most 0.0001.
Values sent between devices are 32-bit elements; how exact they have to be, the bound alone decides.
A program may use at most 32 MiB of HBM per device.

```python
import jax
import jax.numpy as jnp
from jax import lax

LS = 32
NZ = 4
NT = 64
NX = 16
NY = 8


def complex_mul(left_re, left_im, right_re, right_im):
    return (left_re * right_re - left_im * right_im, left_re * right_im + left_im * right_re)


def normalise_row(row_re, row_im):
    factor = lax.rsqrt(jnp.sum(row_re * row_re + row_im * row_im, axis=-1, keepdims=True))
    return (row_re * factor, row_im * factor)


def draw_gauge_links(key, part):
    base_key = jax.random.fold_in(key, 11)
    first_key, second_key = jax.random.split(base_key)
    dims_now = (NX, NY, NZ * NT, 4, 3, 3)
    matrix_re = jax.random.normal(first_key, dims_now, jnp.float32)
    matrix_im = jax.random.normal(second_key, dims_now, jnp.float32)
    first_re, first_im = normalise_row(matrix_re[..., 0, :], matrix_im[..., 0, :])
    second_re = matrix_re[..., 1, :]
    second_im = matrix_im[..., 1, :]
    inner_re = jnp.sum(first_re * second_re + first_im * second_im, axis=-1, keepdims=True)
    inner_im = jnp.sum(first_re * second_im - first_im * second_re, axis=-1, keepdims=True)
    second_re = second_re - (inner_re * first_re - inner_im * first_im)
    second_im = second_im - (inner_re * first_im + inner_im * first_re)
    second_re, second_im = normalise_row(second_re, second_im)
    term_one = complex_mul(jnp.roll(first_re, -1, axis=-1), jnp.roll(first_im, -1, axis=-1), jnp.roll(second_re, -2, axis=-1), jnp.roll(second_im, -2, axis=-1))
    term_two = complex_mul(jnp.roll(first_re, -2, axis=-1), jnp.roll(first_im, -2, axis=-1), jnp.roll(second_re, -1, axis=-1), jnp.roll(second_im, -1, axis=-1))
    third_re = term_one[0] - term_two[0]
    third_im = -(term_one[1] - term_two[1])
    rows_re = jnp.stack([first_re, second_re, third_re], axis=-2)
    rows_im = jnp.stack([first_im, second_im, third_im], axis=-2)
    combined = jnp.stack([rows_re, rows_im], axis=-3)
    combined = jnp.moveaxis(combined, 2, -1)
    return combined.reshape(NX, NY, 72, NZ * NT).astype(jnp.float32)


def levels(rng, shape, cuts, least, largest):
    loudness, own = 1.0, jax.random.fold_in(rng, 6)
    for position, shards_of in cuts:
        draws = jnp.exp(jax.random.uniform(jax.random.fold_in(own, position), (shards_of,), jnp.float32, least / len(cuts), largest / len(cuts)))
        loudness = loudness * jnp.repeat(draws, shape[position] // shards_of).reshape([-1 if axis == position else 1 for axis in range(len(shape))])
    return loudness


def bell_draw(stream_key, dims, scale, bound, cuts=(), kind=jnp.bfloat16):
    entries = jax.random.normal(stream_key, dims, jnp.float32) * scale
    if len(cuts) > 0:
        entries = levels(stream_key, dims, cuts, -0.22, 0.18) * entries
    return jnp.clip(entries, min=-bound, max=bound).astype(kind)


def setup_inputs(seed: int = 0) -> dict:
    streams_of = jax.random.split(jax.random.key(seed), 3)
    return {
        "vectors": bell_draw(streams_of[0], (LS, NX, NY, 24, NZ * NT), 1.0, 6.0, ((0, 32), (1, 8), (2, 4)), jnp.float32),
        "gauge_links": draw_gauge_links(jax.random.fold_in(streams_of[2], 71), 0),
    }


m5_height = 1.8
wall_mass = 0.1
cheb_scale = 0.2
cheb_shift = -0.5
gamma_source = ((3, 2, 1, 0), (3, 2, 1, 0), (2, 3, 0, 1), (2, 3, 0, 1))
gamma_real = ((0, 0, 0, 0), (-1, 1, 1, -1), (0, 0, 0, 0), (1, 1, 1, 1))
gamma_imag = ((-1, -1, 1, 1), (0, 0, 0, 0), (-1, 1, 1, -1), (0, 0, 0, 0))


def split_spin(spinor):
    return spinor.reshape(spinor.shape[:-2] + (4, 2, 3, spinor.shape[-1]))


def join_spin(spinor):
    return spinor.reshape(spinor.shape[:-4] + (24, spinor.shape[-1]))


def gamma_times(spinor, direction, sign):
    pieces = []
    for spin_index in range(4):
        source = spinor[..., gamma_source[direction][spin_index], :, :, :]
        own_spin = spinor[..., spin_index, :, :, :]
        coef_re = sign * gamma_real[direction][spin_index]
        coef_im = sign * gamma_imag[direction][spin_index]
        new_re = own_spin[..., 0, :, :] + coef_re * source[..., 0, :, :] - coef_im * source[..., 1, :, :]
        new_im = own_spin[..., 1, :, :] + coef_re * source[..., 1, :, :] + coef_im * source[..., 0, :, :]
        pieces.append(jnp.stack([new_re, new_im], axis=-3))
    return jnp.stack(pieces, axis=-4)


def colour_times(link_dir, spinor, adjoint):
    link_re = link_dir[:, :, 0]
    link_im = link_dir[:, :, 1]
    if adjoint:
        link_re = jnp.swapaxes(link_re, 2, 3)
        link_im = -jnp.swapaxes(link_im, 2, 3)
    link_re = link_re[None, :, :, None]
    link_im = link_im[None, :, :, None]
    spin_re = spinor[..., 0, :, :][..., None, :, :]
    spin_im = spinor[..., 1, :, :][..., None, :, :]
    out_re = jnp.sum(link_re * spin_re - link_im * spin_im, axis=-2)
    out_im = jnp.sum(link_re * spin_im + link_im * spin_re, axis=-2)
    return jnp.stack([out_re, out_im], axis=-3)


def along_local(spinor, direction, stride):
    local_cells = spinor.shape[-1]
    if direction == 2:
        return jnp.roll(spinor, -stride * NT, axis=-1)
    time_index = jnp.arange(local_cells, dtype=jnp.int32) % NT
    if stride == 1:
        return jnp.where(time_index == NT - 1, -jnp.roll(spinor, NT - 1, axis=-1), jnp.roll(spinor, -1, axis=-1))
    return jnp.where(time_index == 0, -jnp.roll(spinor, 1 - NT, axis=-1), jnp.roll(spinor, 1, axis=-1))


def shift_global(spinor, direction, stride):
    if direction < 2:
        return jnp.roll(spinor, -stride, axis=direction + 1)
    return along_local(spinor, direction, stride)


def hopping(spinor, gauge):
    hop_sum = jnp.zeros_like(spinor)
    for direction in range(4):
        link_dir = gauge[:, :, direction]
        ahead_site = shift_global(spinor, direction, 1)
        forward = colour_times(link_dir, gamma_times(ahead_site, direction, -1), False)
        backward = colour_times(link_dir, gamma_times(spinor, direction, 1), True)
        hop_sum = hop_sum + forward + shift_global(backward, direction, -1)
    return -0.5 * hop_sum


def chiral_hops(spinor):
    slices = jnp.arange(LS, dtype=jnp.int32)[:, None, None, None, None]
    upper_half = jnp.roll(spinor, 1, axis=0)
    upper_half = jnp.where(slices == 0, -wall_mass * upper_half, upper_half)
    lower_half = jnp.roll(spinor, -1, axis=0)
    lower_half = jnp.where(slices == LS - 1, -wall_mass * lower_half, lower_half)
    return jnp.concatenate([upper_half[:, :, :, :12], lower_half[:, :, :, 12:]], axis=3)


def gamma_five(spinor):
    return jnp.concatenate([spinor[:, :, :, :12], -spinor[:, :, :, 12:]], axis=3)


def dirac_operator(spinor, gauge):
    hop_term = join_spin(hopping(split_spin(spinor), gauge))
    return (5.0 - m5_height) * spinor + hop_term - chiral_hops(spinor)


def hermitian(spinor, gauge):
    return gamma_five(dirac_operator(spinor, gauge)[::-1])


def reference(vectors, gauge_links):
    gauge = gauge_links.reshape(gauge_links.shape[:2] + (4, 2, 3, 3, gauge_links.shape[-1]))
    filtered_once = cheb_scale * hermitian(vectors, gauge) + cheb_shift * vectors
    filtered_twice = 2.0 * (cheb_scale * hermitian(filtered_once, gauge) + cheb_shift * filtered_once) - vectors
    return filtered_once, filtered_twice
```

```python
import functools

import jax
import jax.numpy as jnp
from jax import lax
from jax.experimental import pallas as pl
from jax.experimental.pallas import tpu as pltpu
from jax.sharding import PartitionSpec as P

MESH = pl.DeviceIdType.MESH

m5_height = 1.8
wall_mass = 0.1
cheb_scale = 0.2
cheb_shift = -0.5
diagonal = 5.0 - m5_height
source = ((3, 2), (3, 2), (2, 3), (2, 3))
coefficient = (
    ((0, -1), (0, -1), (0, 1), (0, 1)),
    ((-1, 0), (1, 0), (1, 0), (-1, 0)),
    ((0, -1), (0, 1), (0, 1), (0, -1)),
    ((1, 0), (1, 0), (1, 0), (1, 0)),
)
STRIDE = (2, 1)

GY_UP, GY_DOWN, GX_UP, GX_DOWN, SA_UP, SA_DOWN, MIRROR = range(7)


def add_times(base, coef, value):
    re, im = value
    if coef[0] == 1:
        return base[0] + re, base[1] + im
    if coef[0] == -1:
        return base[0] - re, base[1] - im
    if coef[1] == 1:
        return base[0] - im, base[1] + re
    return base[0] + im, base[1] - re


def scaled(coef, sign):
    return coef[0] * sign, coef[1] * sign


def project(field, direction, sign):
    parts = [
        add_times(field(a), scaled(coefficient[direction][a], sign), field(source[direction][a]))
        for a in range(2)
    ]
    return jnp.stack([p[0] for p in parts]), jnp.stack([p[1] for p in parts])


def expand(total, half, direction, sign):
    total = list(total)
    for a in range(2):
        b = source[direction][a]
        value = (half[0][a], half[1][a])
        total[a] = (total[a][0] + value[0], total[a][1] + value[1])
        total[b] = add_times(total[b], scaled(coefficient[direction][b], sign), value)
    return total


def link_of(links, direction):
    base = direction * 18
    re = links[base : base + 9].reshape(3, 3, 8, 128)
    im = links[base + 9 : base + 18].reshape(3, 3, 8, 128)
    return re, im


def link_times(link, half, adjoint):
    re, im = None, None
    for j in range(3):
        u_re = (link[0][j] if adjoint else link[0][:, j])[None]
        u_im = (link[1][j] if adjoint else link[1][:, j])[None]
        h_re, h_im = half[0][:, j][:, None], half[1][:, j][:, None]
        if adjoint:
            t_re = u_re * h_re + u_im * h_im
            t_im = u_re * h_im - u_im * h_re
        else:
            t_re = u_re * h_re - u_im * h_im
            t_im = u_re * h_im + u_im * h_re
        re = t_re if re is None else re + t_re
        im = t_im if im is None else im + t_im
    return re, im


def rolled(value, shift, axis):
    size = value.shape[axis]
    flat = value.reshape((-1,) + value.shape[-2:])
    return pltpu.roll(flat, shift % size, axis + 3).reshape(value.shape)


def masks():
    lane = lax.broadcasted_iota(jnp.int32, (1, 1, 8, 128), 3)
    sub = lax.broadcasted_iota(jnp.int32, (1, 1, 8, 128), 2)
    time = lane % 64
    return {
        "first": time == 0,
        "last": time == 63,
        "zlow": lane < 64,
        "low": tuple((sub // q) % 2 == 0 for q in STRIDE),
    }


def ahead_local(half, direction, mask):
    out = []
    for value in half:
        if direction == 2:
            near = rolled(value, 64, -1)
            out.append(jnp.where(mask["zlow"], near, rolled(near, 4, -2)))
        else:
            out.append(jnp.where(mask["last"], -rolled(value, 63, -1), rolled(value, -1, -1)))
    return out


def behind_local(half, direction, mask):
    out = []
    for value in half:
        if direction == 2:
            near = rolled(value, 64, -1)
            out.append(jnp.where(mask["zlow"], rolled(near, 4, -2), near))
        else:
            out.append(jnp.where(mask["first"], -rolled(value, -63, -1), rolled(value, 1, -1)))
    return out


def kernel(
    v_hbm,
    u_hbm,
    once_ref,
    twice_ref,
    vin,
    uin,
    field_v,
    links,
    field_g,
    mirror_out,
    mirror_in,
    face_out,
    face_in,
    chiral_in,
    local_sem,
    send_sem,
    recv_sem,
):
    axes = ("sa", "gx", "gy")
    me = {axis: lax.axis_index(axis) for axis in axes}
    size = {axis: lax.axis_size(axis) for axis in axes}

    def step(axis, by):
        return {axis: lax.rem(me[axis] + by + size[axis], size[axis])}

    target = {
        GY_UP: step("gy", 1),
        GY_DOWN: step("gy", -1),
        GX_UP: step("gx", 1),
        GX_DOWN: step("gx", -1),
        SA_UP: step("sa", 1),
        SA_DOWN: step("sa", -1),
        MIRROR: {"sa": size["sa"] - 1 - me["sa"]},
    }
    barrier = pltpu.get_barrier_semaphore()
    for device in target.values():
        pl.semaphore_signal(barrier, inc=1, device_id=device, device_id_type=MESH)

    loads = []
    for h in range(2):
        lanes = pl.ds(128 * h, 128)
        loads.append(
            pltpu.make_async_copy(v_hbm.at[:, lanes], vin.at[pl.ds(96 * h, 96)], local_sem.at[h])
        )
        loads.append(
            pltpu.make_async_copy(
                u_hbm.at[:, lanes], uin.at[pl.ds(288 * h, 288)], local_sem.at[2 + h]
            )
        )
    for load in loads:
        load.start()
    for load in loads:
        load.wait()

    for r in range(24):
        field_v[r] = vin[pl.ds(r, 8, stride=24), :]
    for r in range(72):
        links[r] = uin[pl.ds(r, 8, stride=72), :]

    mask = masks()
    copies = {}

    def send(stage, way, src, dst):
        index = stage * 7 + way
        copy = pltpu.make_async_remote_copy(
            src_ref=src,
            dst_ref=dst,
            send_sem=send_sem.at[index],
            recv_sem=recv_sem.at[index],
            device_id=target[way],
            device_id_type=MESH,
        )
        copies[stage, way] = copy
        copy.start()

    def reader(ref):
        def spin(a):
            return ref[a * 6 : a * 6 + 3], ref[a * 6 + 3 : a * 6 + 6]

        return spin

    def faces(field, direction, sign, stage):
        q = STRIDE[direction]
        low = mask["low"][direction]
        up, down = ((GX_UP, GX_DOWN), (GY_UP, GY_DOWN))[direction]
        ahead = project(field, direction, -sign)
        packed = jnp.where(low, ahead[0], rolled(ahead[1], q, -2))
        face_out[stage * 4 + down] = packed.reshape(6, 8, 128)
        behind = link_times(link_of(links, direction), project(field, direction, sign), True)
        packed = jnp.where(low, rolled(behind[1], -q, -2), behind[0])
        face_out[stage * 4 + up] = packed.reshape(6, 8, 128)
        return ahead, behind

    def send_faces(direction, stage):
        for way in ((GX_DOWN, GX_UP), (GY_DOWN, GY_UP))[direction]:
            send(stage, way, face_out.at[stage * 4 + way], face_in.at[stage * 4 + way])

    def hops_local(total, field, sign):
        for direction in (2, 3):
            link = link_of(links, direction)
            ahead = ahead_local(project(field, direction, -sign), direction, mask)
            total = expand(total, link_times(link, ahead, False), direction, -sign)
            behind = link_times(link, project(field, direction, sign), True)
            total = expand(total, behind_local(behind, direction, mask), direction, sign)
        return total

    def hops_across(total, local, direction, sign, stage):
        q = STRIDE[direction]
        low = mask["low"][direction]
        up, down = ((GX_UP, GX_DOWN), (GY_UP, GY_DOWN))[direction]
        ahead, behind = local
        copies[stage, down].wait_recv()
        halo = face_in[stage * 4 + down].reshape(2, 3, 8, 128)
        ahead = (
            jnp.where(low, rolled(ahead[0], -q, -2), rolled(halo, q, -2)),
            jnp.where(low, rolled(ahead[1], -q, -2), halo),
        )
        total = expand(
            total, link_times(link_of(links, direction), ahead, False), direction, -sign
        )
        copies[stage, up].wait_recv()
        halo = face_in[stage * 4 + up].reshape(2, 3, 8, 128)
        behind = (
            jnp.where(low, rolled(halo, -q, -2), rolled(behind[0], q, -2)),
            jnp.where(low, halo, rolled(behind[1], q, -2)),
        )
        return expand(total, behind, direction, sign)

    zero = jnp.zeros((3, 8, 128), jnp.float32)
    nothing = [(zero, zero)] * 4
    last = size["sa"] - 1
    from_down = jnp.where(me["sa"] == 0, -wall_mass, 1.0).astype(jnp.float32)
    from_up = jnp.where(me["sa"] == last, -wall_mass, 1.0).astype(jnp.float32)

    field = reader(field_v)
    local_y = faces(field, 1, 1, 0)
    local_x = faces(field, 0, 1, 0)
    pl.semaphore_wait(barrier, 7)
    send_faces(1, 0)
    send_faces(0, 0)
    send(0, SA_UP, field_v.at[pl.ds(0, 12)], chiral_in.at[pl.ds(0, 12)])
    send(0, SA_DOWN, field_v.at[pl.ds(12, 12)], chiral_in.at[pl.ds(12, 12)])
    total = hops_local(nothing, field, 1)
    total = hops_across(total, local_x, 0, 1, 0)
    total = hops_across(total, local_y, 1, 1, 0)
    copies[0, SA_UP].wait_recv()
    copies[0, SA_DOWN].wait_recv()
    for a in range(4):
        scale = from_down if a < 2 else from_up
        for part in range(2):
            row = a * 6 + part * 3
            value = (
                diagonal * field_v[row : row + 3]
                - 0.5 * total[a][part]
                - scale * chiral_in[row : row + 3]
            )
            field_g[row : row + 3] = value
            for c in range(3):
                mirror_out[pl.ds(row + c, 8, stride=24), :] = value[c]

    send(1, SA_DOWN, field_g.at[pl.ds(0, 12)], chiral_in.at[pl.ds(24, 12)])
    send(1, SA_UP, field_g.at[pl.ds(12, 12)], chiral_in.at[pl.ds(36, 12)])
    send(1, MIRROR, mirror_out, mirror_in)
    field = reader(field_g)
    local_y = faces(field, 1, -1, 1)
    send_faces(1, 1)
    local_x = faces(field, 0, -1, 1)
    send_faces(0, 1)
    total = hops_local(nothing, field, -1)
    total = hops_across(total, local_x, 0, -1, 1)
    total = hops_across(total, local_y, 1, -1, 1)
    copies[1, SA_DOWN].wait_recv()
    copies[1, SA_UP].wait_recv()
    second = 2.0 * cheb_scale * cheb_scale
    for a in range(4):
        scale = from_up if a < 2 else from_down
        for part in range(2):
            row = a * 6 + part * 3
            value = second * (
                diagonal * field_g[row : row + 3]
                - 0.5 * total[a][part]
                - scale * chiral_in[24 + row : 24 + row + 3]
            )
            value = value - 0.5 * field_v[row : row + 3]
            for c in range(3):
                mirror_out_row = pl.ds(row + c, 8, stride=24)
                uin[mirror_out_row, :] = value[c]
    copies[1, MIRROR].wait_recv()
    rows = lax.broadcasted_iota(jnp.int32, (24, 128), 0)
    five = jnp.where(rows < 12, cheb_scale, -cheb_scale).astype(jnp.float32)
    for site in range(4):
        for h in range(2):
            block = pl.ds(h * 96 + site * 24, 24)
            hv = five * mirror_in[block, :]
            place = (pl.ds(site * 24, 24), pl.ds(128 * h, 128))
            once_ref[place] = hv + cheb_shift * vin[block, :]
            twice_ref[place] = uin[block, :] - 2.0 * hv
    for copy in copies.values():
        copy.wait_send()


def per_device(vectors, gauge_links):
    field = vectors.reshape(96, 256)
    links = gauge_links.reshape(288, 256)
    shape = jax.ShapeDtypeStruct((96, 256), jnp.float32)
    once, twice = pl.pallas_call(
        kernel,
        out_shape=(shape, shape),
        in_specs=[pl.BlockSpec(memory_space=pl.ANY)] * 2,
        out_specs=[pl.BlockSpec(memory_space=pltpu.VMEM)] * 2,
        scratch_shapes=[
            pltpu.VMEM((192, 128), jnp.float32),
            pltpu.VMEM((576, 128), jnp.float32),
            pltpu.VMEM((24, 8, 128), jnp.float32),
            pltpu.VMEM((72, 8, 128), jnp.float32),
            pltpu.VMEM((24, 8, 128), jnp.float32),
            pltpu.VMEM((192, 128), jnp.float32),
            pltpu.VMEM((192, 128), jnp.float32),
            pltpu.VMEM((8, 6, 8, 128), jnp.float32),
            pltpu.VMEM((8, 6, 8, 128), jnp.float32),
            pltpu.VMEM((48, 8, 128), jnp.float32),
            pltpu.SemaphoreType.DMA((4,)),
            pltpu.SemaphoreType.DMA((14,)),
            pltpu.SemaphoreType.DMA((14,)),
        ],
        compiler_params=pltpu.CompilerParams(collective_id=0, has_side_effects=True),
        name="chebyshev",
    )(field, links)
    return once.reshape(vectors.shape), twice.reshape(vectors.shape)


def solution(mesh):
    placed = (P("sa", "gx", "gy", None, None), P("gx", "gy", None, None))
    return jax.shard_map(
        per_device,
        mesh=mesh,
        in_specs=placed,
        out_specs=(placed[0], placed[0]),
        check_vma=False,
    )
```

```python
import functools

import jax
import jax.numpy as jnp
from jax import lax
from jax.experimental import pallas as pl
from jax.experimental.pallas import tpu as pltpu
from jax.sharding import PartitionSpec as P

MESH = pl.DeviceIdType.MESH

m5_height = 1.8
wall_mass = 0.1
cheb_scale = 0.2
cheb_shift = -0.5
diagonal = 5.0 - m5_height
source = ((3, 2), (3, 2), (2, 3), (2, 3))
coefficient = (
    ((0, -1), (0, -1), (0, 1), (0, 1)),
    ((-1, 0), (1, 0), (1, 0), (-1, 0)),
    ((0, -1), (0, 1), (0, 1), (0, -1)),
    ((1, 0), (1, 0), (1, 0), (1, 0)),
)
STRIDE = (2, 1)

GY_UP, GY_DOWN, GX_UP, GX_DOWN, SA_UP, SA_DOWN, MIRROR = range(7)


def add_times(base, coef, value):
    re, im = value
    if coef[0] == 1:
        return base[0] + re, base[1] + im
    if coef[0] == -1:
        return base[0] - re, base[1] - im
    if coef[1] == 1:
        return base[0] - im, base[1] + re
    return base[0] + im, base[1] - re


def scaled(coef, sign):
    return coef[0] * sign, coef[1] * sign


def project(field, direction, sign):
    parts = [
        add_times(field(a), scaled(coefficient[direction][a], sign), field(source[direction][a]))
        for a in range(2)
    ]
    return jnp.stack([p[0] for p in parts]), jnp.stack([p[1] for p in parts])


def expand(total, half, direction, sign):
    total = list(total)
    for a in range(2):
        b = source[direction][a]
        value = (half[0][a], half[1][a])
        total[a] = (total[a][0] + value[0], total[a][1] + value[1])
        total[b] = add_times(total[b], scaled(coefficient[direction][b], sign), value)
    return total


def link_of(links, direction):
    base = direction * 18
    re = links[base : base + 9].reshape(3, 3, 8, 128)
    im = links[base + 9 : base + 18].reshape(3, 3, 8, 128)
    return re, im


def link_times(link, half, adjoint):
    re, im = None, None
    for j in range(3):
        u_re = (link[0][j] if adjoint else link[0][:, j])[None]
        u_im = (link[1][j] if adjoint else link[1][:, j])[None]
        h_re, h_im = half[0][:, j][:, None], half[1][:, j][:, None]
        if adjoint:
            t_re = u_re * h_re + u_im * h_im
            t_im = u_re * h_im - u_im * h_re
        else:
            t_re = u_re * h_re - u_im * h_im
            t_im = u_re * h_im + u_im * h_re
        re = t_re if re is None else re + t_re
        im = t_im if im is None else im + t_im
    return re, im


def rolled(value, shift, axis):
    size = value.shape[axis]
    flat = value.reshape((-1,) + value.shape[-2:])
    return pltpu.roll(flat, shift % size, axis + 3).reshape(value.shape)


def masks():
    lane = lax.broadcasted_iota(jnp.int32, (1, 1, 8, 128), 3)
    sub = lax.broadcasted_iota(jnp.int32, (1, 1, 8, 128), 2)
    time = lane % 64
    return {
        "first": time == 0,
        "last": time == 63,
        "zlow": lane < 64,
        "low": tuple((sub // q) % 2 == 0 for q in STRIDE),
    }


def ahead_local(half, direction, mask):
    out = []
    for value in half:
        if direction == 2:
            near = rolled(value, 64, -1)
            out.append(jnp.where(mask["zlow"], near, rolled(near, 4, -2)))
        else:
            out.append(jnp.where(mask["last"], -rolled(value, 63, -1), rolled(value, -1, -1)))
    return out


def behind_local(half, direction, mask):
    out = []
    for value in half:
        if direction == 2:
            near = rolled(value, 64, -1)
            out.append(jnp.where(mask["zlow"], rolled(near, 4, -2), near))
        else:
            out.append(jnp.where(mask["first"], -rolled(value, -63, -1), rolled(value, 1, -1)))
    return out


def kernel(
    v_hbm,
    u_hbm,
    once_ref,
    twice_ref,
    vin,
    uin,
    field_v,
    links,
    field_g,
    mirror_out,
    mirror_in,
    face_out,
    face_in,
    chiral_in,
    local_sem,
    send_sem,
    recv_sem,
):
    axes = ("sa", "gx", "gy")
    me = {axis: lax.axis_index(axis) for axis in axes}
    size = {axis: lax.axis_size(axis) for axis in axes}

    def step(axis, by):
        return {axis: lax.rem(me[axis] + by + size[axis], size[axis])}

    target = {
        GY_UP: step("gy", 1),
        GY_DOWN: step("gy", -1),
        GX_UP: step("gx", 1),
        GX_DOWN: step("gx", -1),
        SA_UP: step("sa", 1),
        SA_DOWN: step("sa", -1),
        MIRROR: {"sa": size["sa"] - 1 - me["sa"]},
    }
    barrier = pltpu.get_barrier_semaphore()
    for device in target.values():
        pl.semaphore_signal(barrier, inc=1, device_id=device, device_id_type=MESH)

    loads = []
    for h in range(2):
        lanes = pl.ds(128 * h, 128)
        loads.append(
            pltpu.make_async_copy(v_hbm.at[:, lanes], vin.at[pl.ds(96 * h, 96)], local_sem.at[h])
        )
        loads.append(
            pltpu.make_async_copy(
                u_hbm.at[:, lanes], uin.at[pl.ds(288 * h, 288)], local_sem.at[2 + h]
            )
        )
    for load in loads:
        load.start()
    for load in loads:
        load.wait()

    for r in range(24):
        field_v[r] = vin[pl.ds(r, 8, stride=24), :]
    for r in range(72):
        links[r] = uin[pl.ds(r, 8, stride=72), :]

    mask = masks()
    copies = {}

    def send(stage, way, src, dst):
        index = stage * 7 + way
        copy = pltpu.make_async_remote_copy(
            src_ref=src,
            dst_ref=dst,
            send_sem=send_sem.at[index],
            recv_sem=recv_sem.at[index],
            device_id=target[way],
            device_id_type=MESH,
        )
        copies[stage, way] = copy
        copy.start()

    def reader(ref):
        def spin(a):
            return ref[a * 6 : a * 6 + 3], ref[a * 6 + 3 : a * 6 + 6]

        return spin

    def faces(field, direction, sign, stage):
        q = STRIDE[direction]
        low = mask["low"][direction]
        up, down = ((GX_UP, GX_DOWN), (GY_UP, GY_DOWN))[direction]
        ahead = project(field, direction, -sign)
        packed = jnp.where(low, ahead[0], rolled(ahead[1], q, -2))
        face_out[stage * 4 + down] = packed.reshape(6, 8, 128)
        behind = link_times(link_of(links, direction), project(field, direction, sign), True)
        packed = jnp.where(low, rolled(behind[1], -q, -2), behind[0])
        face_out[stage * 4 + up] = packed.reshape(6, 8, 128)
        return ahead, behind

    def send_faces(direction, stage):
        for way in ((GX_DOWN, GX_UP), (GY_DOWN, GY_UP))[direction]:
            send(stage, way, face_out.at[stage * 4 + way], face_in.at[stage * 4 + way])

    def hops_local(total, field, sign):
        for direction in (2, 3):
            link = link_of(links, direction)
            ahead = ahead_local(project(field, direction, -sign), direction, mask)
            total = expand(total, link_times(link, ahead, False), direction, -sign)
            behind = link_times(link, project(field, direction, sign), True)
            total = expand(total, behind_local(behind, direction, mask), direction, sign)
        return total

    def hops_across(total, local, direction, sign, stage):
        q = STRIDE[direction]
        low = mask["low"][direction]
        up, down = ((GX_UP, GX_DOWN), (GY_UP, GY_DOWN))[direction]
        ahead, behind = local
        copies[stage, down].wait_recv()
        halo = face_in[stage * 4 + down].reshape(2, 3, 8, 128)
        ahead = (
            jnp.where(low, rolled(ahead[0], -q, -2), rolled(halo, q, -2)),
            jnp.where(low, rolled(ahead[1], -q, -2), halo),
        )
        total = expand(
            total, link_times(link_of(links, direction), ahead, False), direction, -sign
        )
        copies[stage, up].wait_recv()
        halo = face_in[stage * 4 + up].reshape(2, 3, 8, 128)
        behind = (
            jnp.where(low, rolled(halo, -q, -2), rolled(behind[0], q, -2)),
            jnp.where(low, halo, rolled(behind[1], q, -2)),
        )
        return expand(total, behind, direction, sign)

    zero = jnp.zeros((3, 8, 128), jnp.float32)
    nothing = [(zero, zero)] * 4
    last = size["sa"] - 1
    from_down = jnp.where(me["sa"] == 0, -wall_mass, 1.0).astype(jnp.float32)
    from_up = jnp.where(me["sa"] == last, -wall_mass, 1.0).astype(jnp.float32)

    field = reader(field_v)
    local_y = faces(field, 1, 1, 0)
    local_x = faces(field, 0, 1, 0)
    pl.semaphore_wait(barrier, 7)
    send_faces(1, 0)
    send_faces(0, 0)
    send(0, SA_UP, field_v.at[pl.ds(0, 12)], chiral_in.at[pl.ds(0, 12)])
    send(0, SA_DOWN, field_v.at[pl.ds(12, 12)], chiral_in.at[pl.ds(12, 12)])
    total = hops_local(nothing, field, 1)
    total = hops_across(total, local_x, 0, 1, 0)
    total = hops_across(total, local_y, 1, 1, 0)
    copies[0, SA_UP].wait_recv()
    copies[0, SA_DOWN].wait_recv()
    for a in range(4):
        scale = from_down if a < 2 else from_up
        for part in range(2):
            row = a * 6 + part * 3
            value = (
                diagonal * field_v[row : row + 3]
                - 0.5 * total[a][part]
                - scale * chiral_in[row : row + 3]
            )
            field_g[row : row + 3] = value
            for c in range(3):
                mirror_out[pl.ds(row + c, 8, stride=24), :] = value[c]

    send(1, SA_DOWN, field_g.at[pl.ds(0, 12)], chiral_in.at[pl.ds(24, 12)])
    send(1, SA_UP, field_g.at[pl.ds(12, 12)], chiral_in.at[pl.ds(36, 12)])
    send(1, MIRROR, mirror_out, mirror_in)
    field = reader(field_g)
    local_y = faces(field, 1, -1, 1)
    send_faces(1, 1)
    local_x = faces(field, 0, -1, 1)
    send_faces(0, 1)
    total = hops_local(nothing, field, -1)
    total = hops_across(total, local_x, 0, -1, 1)
    total = hops_across(total, local_y, 1, -1, 1)
    copies[1, SA_DOWN].wait_recv()
    copies[1, SA_UP].wait_recv()
    second = 2.0 * cheb_scale * cheb_scale
    for a in range(4):
        scale = from_up if a < 2 else from_down
        for part in range(2):
            row = a * 6 + part * 3
            value = second * (
                diagonal * field_g[row : row + 3]
                - 0.5 * total[a][part]
                - scale * chiral_in[24 + row : 24 + row + 3]
            )
            value = value - 0.5 * field_v[row : row + 3]
            for c in range(3):
                mirror_out_row = pl.ds(row + c, 8, stride=24)
                uin[mirror_out_row, :] = value[c]
    copies[1, MIRROR].wait_recv()
    rows = lax.broadcasted_iota(jnp.int32, (24, 128), 0)
    five = jnp.where(rows < 12, cheb_scale, -cheb_scale).astype(jnp.float32)
    for site in range(4):
        for h in range(2):
            block = pl.ds(h * 96 + site * 24, 24)
            hv = five * mirror_in[block, :]
            place = (pl.ds(site * 24, 24), pl.ds(128 * h, 128))
            once_ref[place] = hv
            twice_ref[place] = uin[block, :]
    for copy in copies.values():
        copy.wait_send()


def per_device(vectors, gauge_links):
    field = vectors.reshape(96, 256)
    links = gauge_links.reshape(288, 256)
    shape = pltpu.VMEM((96, 256), jnp.float32)
    once, twice = pl.pallas_call(
        kernel,
        out_shape=(shape, shape),
        in_specs=[pl.BlockSpec(memory_space=pl.ANY)] * 2,
        out_specs=[pl.BlockSpec(memory_space=pltpu.VMEM)] * 2,
        scratch_shapes=[
            pltpu.VMEM((192, 128), jnp.float32),
            pltpu.VMEM((576, 128), jnp.float32),
            pltpu.VMEM((24, 8, 128), jnp.float32),
            pltpu.VMEM((72, 8, 128), jnp.float32),
            pltpu.VMEM((24, 8, 128), jnp.float32),
            pltpu.VMEM((192, 128), jnp.float32),
            pltpu.VMEM((192, 128), jnp.float32),
            pltpu.VMEM((8, 6, 8, 128), jnp.float32),
            pltpu.VMEM((8, 6, 8, 128), jnp.float32),
            pltpu.VMEM((48, 8, 128), jnp.float32),
            pltpu.SemaphoreType.DMA((4,)),
            pltpu.SemaphoreType.DMA((14,)),
            pltpu.SemaphoreType.DMA((14,)),
        ],
        compiler_params=pltpu.CompilerParams(collective_id=0, has_side_effects=True),
        name="chebyshev",
    )(field, links)
    hv, rest = once, twice
    once = hv + cheb_shift * field
    twice = rest - 2.0 * hv
    return once.reshape(vectors.shape), twice.reshape(vectors.shape)


def solution(mesh):
    placed = (P("sa", "gx", "gy", None, None), P("gx", "gy", None, None))
    return jax.shard_map(
        per_device,
        mesh=mesh,
        in_specs=placed,
        out_specs=(placed[0], placed[0]),
        check_vma=False,
    )
```

```python
import functools

import jax
import jax.numpy as jnp
from jax import lax
from jax.experimental import pallas as pl
from jax.experimental.pallas import tpu as pltpu
from jax.sharding import PartitionSpec as P

MESH = pl.DeviceIdType.MESH

m5_height = 1.8
wall_mass = 0.1
cheb_scale = 0.2
cheb_shift = -0.5
diagonal = 5.0 - m5_height
source = ((3, 2), (3, 2), (2, 3), (2, 3))
coefficient = (
    ((0, -1), (0, -1), (0, 1), (0, 1)),
    ((-1, 0), (1, 0), (1, 0), (-1, 0)),
    ((0, -1), (0, 1), (0, 1), (0, -1)),
    ((1, 0), (1, 0), (1, 0), (1, 0)),
)
STRIDE = (2, 1)

GY_UP, GY_DOWN, GX_UP, GX_DOWN, SA_UP, SA_DOWN, MIRROR = range(7)
BACK = (GY_DOWN, GY_UP, GX_DOWN, GX_UP, SA_DOWN, SA_UP, MIRROR)
MAIN, RELAY_UP, RELAY_DOWN = 12, 13, 14


def add_times(base, coef, value):
    re, im = value
    if coef[0] == 1:
        return base[0] + re, base[1] + im
    if coef[0] == -1:
        return base[0] - re, base[1] - im
    if coef[1] == 1:
        return base[0] - im, base[1] + re
    return base[0] + im, base[1] - re


def scaled(coef, sign):
    return coef[0] * sign, coef[1] * sign


def project(field, direction, sign):
    parts = [
        add_times(field(a), scaled(coefficient[direction][a], sign), field(source[direction][a]))
        for a in range(2)
    ]
    return jnp.stack([p[0] for p in parts]), jnp.stack([p[1] for p in parts])


def expand(total, half, direction, sign):
    total = list(total)
    for a in range(2):
        b = source[direction][a]
        value = (half[0][a], half[1][a])
        total[a] = (total[a][0] + value[0], total[a][1] + value[1])
        total[b] = add_times(total[b], scaled(coefficient[direction][b], sign), value)
    return total


def link_of(links, direction):
    base = direction * 18
    re = links[base : base + 9].reshape(3, 3, 8, 128)
    im = links[base + 9 : base + 18].reshape(3, 3, 8, 128)
    return re, im


def link_times(link, half, adjoint):
    re, im = None, None
    for j in range(3):
        u_re = (link[0][j] if adjoint else link[0][:, j])[None]
        u_im = (link[1][j] if adjoint else link[1][:, j])[None]
        h_re, h_im = half[0][:, j][:, None], half[1][:, j][:, None]
        if adjoint:
            t_re = u_re * h_re + u_im * h_im
            t_im = u_re * h_im - u_im * h_re
        else:
            t_re = u_re * h_re - u_im * h_im
            t_im = u_re * h_im + u_im * h_re
        re = t_re if re is None else re + t_re
        im = t_im if im is None else im + t_im
    return re, im


def rolled(value, shift, axis):
    size = value.shape[axis]
    flat = value.reshape((-1,) + value.shape[-2:])
    return pltpu.roll(flat, shift % size, axis + 3).reshape(value.shape)


def masks():
    lane = lax.broadcasted_iota(jnp.int32, (1, 1, 8, 128), 3)
    sub = lax.broadcasted_iota(jnp.int32, (1, 1, 8, 128), 2)
    time = lane % 64
    return {
        "first": time == 0,
        "last": time == 63,
        "zlow": lane < 64,
        "low": tuple((sub // q) % 2 == 0 for q in STRIDE),
    }


def ahead_local(half, direction, mask):
    out = []
    for value in half:
        if direction == 2:
            near = rolled(value, 64, -1)
            out.append(jnp.where(mask["zlow"], near, rolled(near, 4, -2)))
        else:
            out.append(jnp.where(mask["last"], -rolled(value, 63, -1), rolled(value, -1, -1)))
    return out


def behind_local(half, direction, mask):
    out = []
    for value in half:
        if direction == 2:
            near = rolled(value, 64, -1)
            out.append(jnp.where(mask["zlow"], rolled(near, 4, -2), near))
        else:
            out.append(jnp.where(mask["first"], -rolled(value, -63, -1), rolled(value, 1, -1)))
    return out


def kernel(
    v_hbm,
    u_hbm,
    mirrored_ref,
    rest_ref,
    vin,
    uin,
    field_v,
    links,
    field_p,
    field_g,
    face_out,
    face_in,
    chiral_in,
    mirror_in,
    relay_in,
    natural,
    local_sem,
    known_sem,
    send_sem,
    recv_sem,
):
    axes = ("sa", "gx", "gy")
    me = {axis: lax.axis_index(axis) for axis in axes}
    size = {axis: lax.axis_size(axis) for axis in axes}

    def step(axis, by):
        return {axis: lax.rem(me[axis] + by + size[axis], size[axis])}

    target = (
        step("gy", 1),
        step("gy", -1),
        step("gx", 1),
        step("gx", -1),
        step("sa", 1),
        step("sa", -1),
        {"sa": size["sa"] - 1 - me["sa"]},
    )

    def rank(axis, index):
        return index + 1 - 2 * lax.rem(index, 2) if axis == "gx" else index

    first = []
    lowest = me["gy"] == 0
    for way, device in enumerate(target):
        ((axis, index),) = device.items()
        ahead = rank(axis, me[axis]) < rank(axis, index)
        if way in (SA_UP, SA_DOWN):
            wraps = jnp.abs(me[axis] - index) == size[axis] - 1
            ahead = jnp.logical_xor(ahead, jnp.logical_and(lowest, wraps))
        first.append(ahead)
    barrier = pltpu.get_barrier_semaphore()
    for way, device in enumerate(target):

        @pl.when(first[way])
        def _(device=device):
            pl.semaphore_signal(barrier, inc=1, device_id=device, device_id_type=MESH)

    loads = []
    for h in range(2):
        lanes = pl.ds(128 * h, 128)
        loads.append(
            pltpu.make_async_copy(v_hbm.at[:, lanes], vin.at[pl.ds(96 * h, 96)], local_sem.at[h])
        )
        loads.append(
            pltpu.make_async_copy(
                u_hbm.at[:, lanes], uin.at[pl.ds(288 * h, 288)], local_sem.at[2 + h]
            )
        )
    for load in loads:
        load.start()

    copies = {}

    def copy_of(index, way, src, dst):
        copies[index] = pltpu.make_async_remote_copy(
            src_ref=src,
            dst_ref=dst,
            send_sem=send_sem.at[index],
            recv_sem=recv_sem.at[index],
            device_id=target[way],
            device_id_type=MESH,
        )
        return copies[index]

    def meet(way):
        @pl.when(first[way])
        def _():
            pl.semaphore_wait(known_sem.at[way], 1)

    for stage in range(2):
        for way in (GY_UP, GY_DOWN, GX_UP, GX_DOWN):
            slot = stage * 4 + way
            copy_of(stage * 6 + way, way, face_out.at[slot], face_in.at[slot])
    upper, lower = pl.ds(0, 12), pl.ds(12, 12)
    copy_of(SA_UP, SA_UP, field_v.at[upper], chiral_in.at[pl.ds(0, 12)])
    copy_of(SA_DOWN, SA_DOWN, field_v.at[lower], chiral_in.at[pl.ds(12, 12)])
    copy_of(6 + SA_DOWN, SA_DOWN, field_g.at[upper], chiral_in.at[pl.ds(24, 12)])
    copy_of(6 + SA_UP, SA_UP, field_g.at[lower], chiral_in.at[pl.ds(36, 12)])
    copy_of(MAIN, MIRROR, field_p, mirror_in)
    copy_of(RELAY_UP, MIRROR, face_in.at[GY_DOWN], relay_in.at[0])
    copy_of(RELAY_DOWN, MIRROR, face_in.at[GY_UP], relay_in.at[1])

    mask = masks()
    zero = jnp.zeros((3, 8, 128), jnp.float32)
    nothing = [(zero, zero)] * 4

    def reader(ref):
        def spin(a):
            return ref[a * 6 : a * 6 + 3], ref[a * 6 + 3 : a * 6 + 6]

        return spin

    def halves(field, direction, sign):
        ahead = project(field, direction, -sign)
        behind = link_times(link_of(links, direction), project(field, direction, sign), True)
        return ahead, behind

    def pack(pair, direction, stage):
        q = STRIDE[direction]
        low = mask["low"][direction]
        up, down = ((GX_UP, GX_DOWN), (GY_UP, GY_DOWN))[direction]
        ahead, behind = pair
        packed = jnp.where(low, ahead[0], rolled(ahead[1], q, -2))
        face_out[stage * 4 + down] = packed.reshape(6, 8, 128)
        packed = jnp.where(low, rolled(behind[1], -q, -2), behind[0])
        face_out[stage * 4 + up] = packed.reshape(6, 8, 128)

    def unpack(from_up, from_down, direction):
        q = STRIDE[direction]
        from_up = from_up.reshape(2, 3, 8, 128)
        from_down = from_down.reshape(2, 3, 8, 128)
        return (rolled(from_up, q, -2), from_up), (rolled(from_down, -q, -2), from_down)

    def hops_local(total, field, sign):
        for direction in (2, 3):
            link = link_of(links, direction)
            ahead = ahead_local(project(field, direction, -sign), direction, mask)
            total = expand(total, link_times(link, ahead, False), direction, -sign)
            behind = link_times(link, project(field, direction, sign), True)
            total = expand(total, behind_local(behind, direction, mask), direction, sign)
        return total

    def hops_across(total, pair, halo, direction, sign):
        q = STRIDE[direction]
        low = mask["low"][direction]
        ahead, behind = pair
        ahead = [jnp.where(low, rolled(ahead[k], -q, -2), halo[0][k]) for k in range(2)]
        behind = [jnp.where(low, halo[1][k], rolled(behind[k], q, -2)) for k in range(2)]
        link = link_of(links, direction)
        total = expand(total, link_times(link, ahead, False), direction, -sign)
        return expand(total, behind, direction, sign)

    def halo_terms(halo):
        low = mask["low"][1]
        ahead = [jnp.where(low, 0.0, halo[0][k]) for k in range(2)]
        behind = [jnp.where(low, halo[1][k], 0.0) for k in range(2)]
        total = expand(nothing, link_times(link_of(links, 1), ahead, False), 1, -1)
        return expand(total, behind, 1, 1)

    last = size["sa"] - 1
    from_down = jnp.where(me["sa"] == 0, -wall_mass, 1.0).astype(jnp.float32)
    from_up = jnp.where(me["sa"] == last, -wall_mass, 1.0).astype(jnp.float32)
    no_halo = ((0.0, 0.0), (0.0, 0.0))

    for load in loads:
        load.wait()
    for r in range(24):
        field_v[r] = vin[pl.ds(r, 8, stride=24), :]
    for r in range(72):
        links[r] = uin[pl.ds(r, 8, stride=72), :]

    field = reader(field_v)
    pair_y = halves(field, 1, 1)
    pack(pair_y, 1, 0)
    pair_x = halves(field, 0, 1)
    pack(pair_x, 0, 0)

    count = jnp.int32(0)
    for way in range(7):
        count = count + jnp.where(first[way], 0, 1)
    pl.semaphore_wait(barrier, count)
    for way in (GY_UP, GY_DOWN):

        @pl.when(jnp.logical_not(first[way]))
        def _(way=way):
            copies[way].start()

    for way, device in enumerate(target):

        @pl.when(jnp.logical_not(first[way]))
        def _(way=way, device=device):
            pl.semaphore_signal(
                known_sem.at[BACK[way]], inc=1, device_id=device, device_id_type=MESH
            )

    for way in (GX_DOWN, GX_UP, SA_UP, SA_DOWN):
        meet(way)
        copies[way].start()
    total = hops_local(nothing, field, 1)
    total = hops_across(total, pair_y, no_halo, 1, 1)
    copies[GX_DOWN].wait_recv()
    copies[GX_UP].wait_recv()
    halo = unpack(face_in[GX_DOWN], face_in[GX_UP], 0)
    total = hops_across(total, pair_x, halo, 0, 1)
    copies[SA_UP].wait_recv()
    copies[SA_DOWN].wait_recv()
    for a in range(4):
        scale = from_down if a < 2 else from_up
        for part in range(2):
            row = a * 6 + part * 3
            field_p[row : row + 3] = (
                diagonal * field_v[row : row + 3]
                - 0.5 * total[a][part]
                - scale * chiral_in[row : row + 3]
            )
    meet(MIRROR)
    copies[MAIN].start()
    pack(halves(reader(field_p), 1, -1), 1, 1)
    for way in (GY_UP, GY_DOWN):

        @pl.when(jnp.logical_not(first[way]))
        def _(way=way):
            copies[6 + way].start()

    for way, relay in ((GY_UP, RELAY_UP), (GY_DOWN, RELAY_DOWN)):

        @pl.when(first[way])
        def _(way=way):
            pl.semaphore_wait(known_sem.at[way], 1)
            copies[way].start()
            copies[6 + way].start()

        copies[BACK[way]].wait_recv()
        copies[relay].start()

    halo = unpack(face_in[GY_DOWN], face_in[GY_UP], 1)
    total = halo_terms(halo)
    for a in range(4):
        for part in range(2):
            row = a * 6 + part * 3
            field_g[row : row + 3] = field_p[row : row + 3] - 0.5 * total[a][part]
    copies[6 + SA_DOWN].start()
    copies[6 + SA_UP].start()
    field = reader(field_g)
    pair_x = halves(field, 0, -1)
    pack(pair_x, 0, 1)
    copies[6 + GX_DOWN].start()
    copies[6 + GX_UP].start()
    total = hops_local(nothing, field, -1)
    copies[6 + GY_DOWN].wait_recv()
    copies[6 + GY_UP].wait_recv()
    halo = unpack(face_in[4 + GY_DOWN], face_in[4 + GY_UP], 1)
    halo = (
        [halo[0][k] - pair_y[1][k] for k in range(2)],
        [halo[1][k] - pair_y[0][k] for k in range(2)],
    )
    total = hops_across(total, halves(field, 1, -1), halo, 1, -1)
    copies[6 + GX_DOWN].wait_recv()
    copies[6 + GX_UP].wait_recv()
    halo = unpack(face_in[4 + GX_DOWN], face_in[4 + GX_UP], 0)
    total = hops_across(total, pair_x, halo, 0, -1)
    copies[6 + SA_DOWN].wait_recv()
    copies[6 + SA_UP].wait_recv()
    second = 2.0 * cheb_scale * cheb_scale

    def spread(ref):
        for site in range(4):
            for h in range(2):
                block = pl.ds(h * 96 + site * 24, 24)
                ref[pl.ds(site * 24, 24), pl.ds(128 * h, 128)] = natural[block, :]

    for a in range(4):
        scale = from_up if a < 2 else from_down
        for part in range(2):
            row = a * 6 + part * 3
            value = second * (
                diagonal * field_g[row : row + 3]
                - 0.5 * total[a][part]
                - scale * chiral_in[24 + row : 24 + row + 3]
            )
            value = value + cheb_shift * field_v[row : row + 3]
            for c in range(3):
                natural[pl.ds(row + c, 8, stride=24), :] = value[c]
    spread(rest_ref)
    for index in (MAIN, RELAY_UP, RELAY_DOWN):
        copies[index].wait_recv()
    total = halo_terms(unpack(relay_in[0], relay_in[1], 1))
    for a in range(4):
        scale = cheb_scale if a < 2 else -cheb_scale
        for part in range(2):
            row = a * 6 + part * 3
            value = scale * (mirror_in[row : row + 3] - 0.5 * total[a][part])
            for c in range(3):
                natural[pl.ds(row + c, 8, stride=24), :] = value[c]
    spread(mirrored_ref)
    for copy in copies.values():
        copy.wait_send()


def per_device(vectors, gauge_links):
    field = vectors.reshape(96, 256)
    links = gauge_links.reshape(288, 256)
    shape = pltpu.VMEM((96, 256), jnp.float32)
    once, twice = pl.pallas_call(
        kernel,
        out_shape=(shape, shape),
        in_specs=[pl.BlockSpec(memory_space=pl.ANY)] * 2,
        out_specs=[pl.BlockSpec(memory_space=pltpu.VMEM)] * 2,
        scratch_shapes=[
            pltpu.VMEM((192, 128), jnp.float32),
            pltpu.VMEM((576, 128), jnp.float32),
            pltpu.VMEM((24, 8, 128), jnp.float32),
            pltpu.VMEM((72, 8, 128), jnp.float32),
            pltpu.VMEM((24, 8, 128), jnp.float32),
            pltpu.VMEM((24, 8, 128), jnp.float32),
            pltpu.VMEM((8, 6, 8, 128), jnp.float32),
            pltpu.VMEM((8, 6, 8, 128), jnp.float32),
            pltpu.VMEM((48, 8, 128), jnp.float32),
            pltpu.VMEM((24, 8, 128), jnp.float32),
            pltpu.VMEM((2, 6, 8, 128), jnp.float32),
            pltpu.VMEM((192, 128), jnp.float32),
            pltpu.SemaphoreType.DMA((4,)),
            pltpu.SemaphoreType.REGULAR((7,)),
            pltpu.SemaphoreType.DMA((15,)),
            pltpu.SemaphoreType.DMA((15,)),
        ],
        compiler_params=pltpu.CompilerParams(collective_id=0, has_side_effects=True),
        name="chebyshev",
    )(field, links)
    hv, rest = once, twice
    once = hv + cheb_shift * field
    twice = rest - 2.0 * hv
    return once.reshape(vectors.shape), twice.reshape(vectors.shape)


def solution(mesh):
    placed = (P("sa", "gx", "gy", None, None), P("gx", "gy", None, None))
    return jax.shard_map(
        per_device,
        mesh=mesh,
        in_specs=placed,
        out_specs=(placed[0], placed[0]),
        check_vma=False,
    )
```

```python
import functools

import jax
import jax.numpy as jnp
from jax import lax
from jax.experimental import pallas as pl
from jax.experimental.pallas import tpu as pltpu
from jax.sharding import PartitionSpec as P

MESH = pl.DeviceIdType.MESH

m5_height = 1.8
wall_mass = 0.1
cheb_scale = 0.2
cheb_shift = -0.5
diagonal = 5.0 - m5_height
source = ((3, 2), (3, 2), (2, 3), (2, 3))
coefficient = (
    ((0, -1), (0, -1), (0, 1), (0, 1)),
    ((-1, 0), (1, 0), (1, 0), (-1, 0)),
    ((0, -1), (0, 1), (0, 1), (0, -1)),
    ((1, 0), (1, 0), (1, 0), (1, 0)),
)
STRIDE = (2, 1)

GY_UP, GY_DOWN, GX_UP, GX_DOWN, SA_UP, SA_DOWN, MIRROR = range(7)
BACK = (GY_DOWN, GY_UP, GX_DOWN, GX_UP, SA_DOWN, SA_UP, MIRROR)
MAIN, RELAY_UP, RELAY_DOWN = 12, 13, 14


def add_times(base, coef, value):
    re, im = value
    if coef[0] == 1:
        return base[0] + re, base[1] + im
    if coef[0] == -1:
        return base[0] - re, base[1] - im
    if coef[1] == 1:
        return base[0] - im, base[1] + re
    return base[0] + im, base[1] - re


def scaled(coef, sign):
    return coef[0] * sign, coef[1] * sign


def project(field, direction, sign):
    parts = [
        add_times(field(a), scaled(coefficient[direction][a], sign), field(source[direction][a]))
        for a in range(2)
    ]
    return jnp.stack([p[0] for p in parts]), jnp.stack([p[1] for p in parts])


def expand(total, half, direction, sign):
    total = list(total)
    for a in range(2):
        b = source[direction][a]
        value = (half[0][a], half[1][a])
        total[a] = (total[a][0] + value[0], total[a][1] + value[1])
        total[b] = add_times(total[b], scaled(coefficient[direction][b], sign), value)
    return total


def link_of(links, direction):
    base = direction * 18
    re = links[base : base + 9].reshape(3, 3, 8, 128)
    im = links[base + 9 : base + 18].reshape(3, 3, 8, 128)
    return re, im


def link_times(link, half, adjoint):
    re, im = None, None
    for j in range(3):
        u_re = (link[0][j] if adjoint else link[0][:, j])[None]
        u_im = (link[1][j] if adjoint else link[1][:, j])[None]
        h_re, h_im = half[0][:, j][:, None], half[1][:, j][:, None]
        if adjoint:
            t_re = u_re * h_re + u_im * h_im
            t_im = u_re * h_im - u_im * h_re
        else:
            t_re = u_re * h_re - u_im * h_im
            t_im = u_re * h_im + u_im * h_re
        re = t_re if re is None else re + t_re
        im = t_im if im is None else im + t_im
    return re, im


def rolled(value, shift, axis):
    size = value.shape[axis]
    flat = value.reshape((-1,) + value.shape[-2:])
    return pltpu.roll(flat, shift % size, axis + 3).reshape(value.shape)


def masks():
    lane = lax.broadcasted_iota(jnp.int32, (1, 1, 8, 128), 3)
    sub = lax.broadcasted_iota(jnp.int32, (1, 1, 8, 128), 2)
    time = lane % 64
    return {
        "first": time == 0,
        "last": time == 63,
        "zlow": lane < 64,
        "low": tuple((sub // q) % 2 == 0 for q in STRIDE),
    }


def ahead_local(half, direction, mask):
    out = []
    for value in half:
        if direction == 2:
            near = rolled(value, 64, -1)
            out.append(jnp.where(mask["zlow"], near, rolled(near, 4, -2)))
        else:
            out.append(jnp.where(mask["last"], -rolled(value, 63, -1), rolled(value, -1, -1)))
    return out


def behind_local(half, direction, mask):
    out = []
    for value in half:
        if direction == 2:
            near = rolled(value, 64, -1)
            out.append(jnp.where(mask["zlow"], rolled(near, 4, -2), near))
        else:
            out.append(jnp.where(mask["first"], -rolled(value, -63, -1), rolled(value, 1, -1)))
    return out


def kernel(
    v_hbm,
    u_hbm,
    mirrored_ref,
    rest_ref,
    vin,
    uin,
    field_v,
    links,
    field_p,
    field_g,
    face_out,
    face_in,
    chiral_in,
    mirror_in,
    relay_in,
    natural,
    local_sem,
    known_sem,
    send_sem,
    recv_sem,
):
    axes = ("sa", "gx", "gy")
    me = {axis: lax.axis_index(axis) for axis in axes}
    size = {axis: lax.axis_size(axis) for axis in axes}

    def step(axis, by):
        return {axis: lax.rem(me[axis] + by + size[axis], size[axis])}

    target = (
        step("gy", 1),
        step("gy", -1),
        step("gx", 1),
        step("gx", -1),
        step("sa", 1),
        step("sa", -1),
        {"sa": size["sa"] - 1 - me["sa"]},
    )

    def rank(axis, index):
        if axis == "gx":
            return index + 1 - 2 * lax.rem(index, 2)
        if axis == "gy":
            return jnp.where(index < 2, index, 5 - index)
        return index

    first = []
    lowest = me["gy"] == 0
    for way, device in enumerate(target):
        ((axis, index),) = device.items()
        ahead = rank(axis, me[axis]) < rank(axis, index)
        if way in (SA_UP, SA_DOWN):
            wraps = jnp.abs(me[axis] - index) == size[axis] - 1
            ahead = jnp.logical_xor(ahead, jnp.logical_and(lowest, wraps))
        first.append(ahead)
    barrier = pltpu.get_barrier_semaphore()
    for way, device in enumerate(target):

        @pl.when(first[way])
        def _(device=device):
            pl.semaphore_signal(barrier, inc=1, device_id=device, device_id_type=MESH)

    loads = []
    for h in range(2):
        lanes = pl.ds(128 * h, 128)
        loads.append(
            pltpu.make_async_copy(v_hbm.at[:, lanes], vin.at[pl.ds(96 * h, 96)], local_sem.at[h])
        )
        loads.append(
            pltpu.make_async_copy(
                u_hbm.at[:, lanes], uin.at[pl.ds(288 * h, 288)], local_sem.at[2 + h]
            )
        )
    for load in loads:
        load.start()

    copies = {}

    def copy_of(index, way, src, dst):
        copies[index] = pltpu.make_async_remote_copy(
            src_ref=src,
            dst_ref=dst,
            send_sem=send_sem.at[index],
            recv_sem=recv_sem.at[index],
            device_id=target[way],
            device_id_type=MESH,
        )
        return copies[index]

    def meet(way):
        @pl.when(first[way])
        def _():
            pl.semaphore_wait(known_sem.at[way], 1)

    for stage in range(2):
        for way in (GY_UP, GY_DOWN, GX_UP, GX_DOWN):
            slot = stage * 4 + way
            copy_of(stage * 6 + way, way, face_out.at[slot], face_in.at[slot])
    upper, lower = pl.ds(0, 12), pl.ds(12, 12)
    copy_of(SA_UP, SA_UP, field_v.at[upper], chiral_in.at[pl.ds(0, 12)])
    copy_of(SA_DOWN, SA_DOWN, field_v.at[lower], chiral_in.at[pl.ds(12, 12)])
    copy_of(6 + SA_DOWN, SA_DOWN, field_g.at[upper], chiral_in.at[pl.ds(24, 12)])
    copy_of(6 + SA_UP, SA_UP, field_g.at[lower], chiral_in.at[pl.ds(36, 12)])
    copy_of(MAIN, MIRROR, field_p, mirror_in)
    copy_of(RELAY_UP, MIRROR, face_in.at[GY_DOWN], relay_in.at[0])
    copy_of(RELAY_DOWN, MIRROR, face_in.at[GY_UP], relay_in.at[1])

    mask = masks()
    zero = jnp.zeros((3, 8, 128), jnp.float32)
    nothing = [(zero, zero)] * 4

    def reader(ref):
        def spin(a):
            return ref[a * 6 : a * 6 + 3], ref[a * 6 + 3 : a * 6 + 6]

        return spin

    def halves(field, direction, sign):
        ahead = project(field, direction, -sign)
        behind = link_times(link_of(links, direction), project(field, direction, sign), True)
        return ahead, behind

    def pack(pair, direction, stage):
        q = STRIDE[direction]
        low = mask["low"][direction]
        up, down = ((GX_UP, GX_DOWN), (GY_UP, GY_DOWN))[direction]
        ahead, behind = pair
        packed = jnp.where(low, ahead[0], rolled(ahead[1], q, -2))
        face_out[stage * 4 + down] = packed.reshape(6, 8, 128)
        packed = jnp.where(low, rolled(behind[1], -q, -2), behind[0])
        face_out[stage * 4 + up] = packed.reshape(6, 8, 128)

    def unpack(from_up, from_down, direction):
        q = STRIDE[direction]
        from_up = from_up.reshape(2, 3, 8, 128)
        from_down = from_down.reshape(2, 3, 8, 128)
        return (rolled(from_up, q, -2), from_up), (rolled(from_down, -q, -2), from_down)

    def hops_local(total, field, sign):
        for direction in (2, 3):
            link = link_of(links, direction)
            ahead = ahead_local(project(field, direction, -sign), direction, mask)
            total = expand(total, link_times(link, ahead, False), direction, -sign)
            behind = link_times(link, project(field, direction, sign), True)
            total = expand(total, behind_local(behind, direction, mask), direction, sign)
        return total

    def hops_across(total, pair, halo, direction, sign):
        q = STRIDE[direction]
        low = mask["low"][direction]
        ahead, behind = pair
        ahead = [jnp.where(low, rolled(ahead[k], -q, -2), halo[0][k]) for k in range(2)]
        behind = [jnp.where(low, halo[1][k], rolled(behind[k], q, -2)) for k in range(2)]
        link = link_of(links, direction)
        total = expand(total, link_times(link, ahead, False), direction, -sign)
        return expand(total, behind, direction, sign)

    def halo_terms(halo):
        low = mask["low"][1]
        ahead = [jnp.where(low, 0.0, halo[0][k]) for k in range(2)]
        behind = [jnp.where(low, halo[1][k], 0.0) for k in range(2)]
        total = expand(nothing, link_times(link_of(links, 1), ahead, False), 1, -1)
        return expand(total, behind, 1, 1)

    last = size["sa"] - 1
    from_down = jnp.where(me["sa"] == 0, -wall_mass, 1.0).astype(jnp.float32)
    from_up = jnp.where(me["sa"] == last, -wall_mass, 1.0).astype(jnp.float32)
    no_halo = ((0.0, 0.0), (0.0, 0.0))

    for load in loads:
        load.wait()
    for r in range(24):
        field_v[r] = vin[pl.ds(r, 8, stride=24), :]
    for r in range(72):
        links[r] = uin[pl.ds(r, 8, stride=72), :]

    field = reader(field_v)
    pair_y = halves(field, 1, 1)
    pack(pair_y, 1, 0)
    pair_x = halves(field, 0, 1)
    pack(pair_x, 0, 0)

    count = jnp.int32(0)
    for way in range(7):
        count = count + jnp.where(first[way], 0, 1)
    pl.semaphore_wait(barrier, count)
    for way in (GY_UP, GY_DOWN):

        @pl.when(jnp.logical_not(first[way]))
        def _(way=way):
            copies[way].start()

    for way, device in enumerate(target):

        @pl.when(jnp.logical_not(first[way]))
        def _(way=way, device=device):
            pl.semaphore_signal(
                known_sem.at[BACK[way]], inc=1, device_id=device, device_id_type=MESH
            )

    for way in (GX_DOWN, GX_UP, SA_UP, SA_DOWN):
        meet(way)
        copies[way].start()
    total = hops_local(nothing, field, 1)
    total = hops_across(total, pair_y, no_halo, 1, 1)
    copies[GX_DOWN].wait_recv()
    copies[GX_UP].wait_recv()
    halo = unpack(face_in[GX_DOWN], face_in[GX_UP], 0)
    total = hops_across(total, pair_x, halo, 0, 1)
    copies[SA_UP].wait_recv()
    copies[SA_DOWN].wait_recv()
    for a in range(4):
        scale = from_down if a < 2 else from_up
        for part in range(2):
            row = a * 6 + part * 3
            field_p[row : row + 3] = (
                diagonal * field_v[row : row + 3]
                - 0.5 * total[a][part]
                - scale * chiral_in[row : row + 3]
            )
    meet(MIRROR)
    copies[MAIN].start()
    pack(halves(reader(field_p), 1, -1), 1, 1)
    for way in (GY_UP, GY_DOWN):

        @pl.when(jnp.logical_not(first[way]))
        def _(way=way):
            copies[6 + way].start()

    for way, relay in ((GY_UP, RELAY_UP), (GY_DOWN, RELAY_DOWN)):

        @pl.when(first[way])
        def _(way=way):
            pl.semaphore_wait(known_sem.at[way], 1)
            copies[way].start()
            copies[6 + way].start()

        copies[BACK[way]].wait_recv()
        copies[relay].start()

    halo = unpack(face_in[GY_DOWN], face_in[GY_UP], 1)
    total = halo_terms(halo)
    for a in range(4):
        for part in range(2):
            row = a * 6 + part * 3
            field_g[row : row + 3] = field_p[row : row + 3] - 0.5 * total[a][part]
    copies[6 + SA_DOWN].start()
    copies[6 + SA_UP].start()
    field = reader(field_g)
    pair_x = halves(field, 0, -1)
    pack(pair_x, 0, 1)
    copies[6 + GX_DOWN].start()
    copies[6 + GX_UP].start()
    total = hops_local(nothing, field, -1)
    copies[6 + GY_DOWN].wait_recv()
    copies[6 + GY_UP].wait_recv()
    halo = unpack(face_in[4 + GY_DOWN], face_in[4 + GY_UP], 1)
    halo = (
        [halo[0][k] - pair_y[1][k] for k in range(2)],
        [halo[1][k] - pair_y[0][k] for k in range(2)],
    )
    total = hops_across(total, halves(field, 1, -1), halo, 1, -1)
    copies[6 + GX_DOWN].wait_recv()
    copies[6 + GX_UP].wait_recv()
    halo = unpack(face_in[4 + GX_DOWN], face_in[4 + GX_UP], 0)
    total = hops_across(total, pair_x, halo, 0, -1)
    copies[6 + SA_DOWN].wait_recv()
    copies[6 + SA_UP].wait_recv()
    second = 2.0 * cheb_scale * cheb_scale

    def spread(ref):
        for site in range(4):
            for h in range(2):
                block = pl.ds(h * 96 + site * 24, 24)
                ref[pl.ds(site * 24, 24), pl.ds(128 * h, 128)] = natural[block, :]

    for a in range(4):
        scale = from_up if a < 2 else from_down
        for part in range(2):
            row = a * 6 + part * 3
            value = second * (
                diagonal * field_g[row : row + 3]
                - 0.5 * total[a][part]
                - scale * chiral_in[24 + row : 24 + row + 3]
            )
            value = value + cheb_shift * field_v[row : row + 3]
            for c in range(3):
                natural[pl.ds(row + c, 8, stride=24), :] = value[c]
    spread(rest_ref)
    for index in (MAIN, RELAY_UP, RELAY_DOWN):
        copies[index].wait_recv()
    total = halo_terms(unpack(relay_in[0], relay_in[1], 1))
    for a in range(4):
        scale = cheb_scale if a < 2 else -cheb_scale
        for part in range(2):
            row = a * 6 + part * 3
            value = scale * (mirror_in[row : row + 3] - 0.5 * total[a][part])
            for c in range(3):
                natural[pl.ds(row + c, 8, stride=24), :] = value[c]
    spread(mirrored_ref)
    for copy in copies.values():
        copy.wait_send()


def per_device(vectors, gauge_links):
    field = vectors.reshape(96, 256)
    links = gauge_links.reshape(288, 256)
    shape = pltpu.VMEM((96, 256), jnp.float32)
    once, twice = pl.pallas_call(
        kernel,
        out_shape=(shape, shape),
        in_specs=[pl.BlockSpec(memory_space=pl.ANY)] * 2,
        out_specs=[pl.BlockSpec(memory_space=pltpu.VMEM)] * 2,
        scratch_shapes=[
            pltpu.VMEM((192, 128), jnp.float32),
            pltpu.VMEM((576, 128), jnp.float32),
            pltpu.VMEM((24, 8, 128), jnp.float32),
            pltpu.VMEM((72, 8, 128), jnp.float32),
            pltpu.VMEM((24, 8, 128), jnp.float32),
            pltpu.VMEM((24, 8, 128), jnp.float32),
            pltpu.VMEM((8, 6, 8, 128), jnp.float32),
            pltpu.VMEM((8, 6, 8, 128), jnp.float32),
            pltpu.VMEM((48, 8, 128), jnp.float32),
            pltpu.VMEM((24, 8, 128), jnp.float32),
            pltpu.VMEM((2, 6, 8, 128), jnp.float32),
            pltpu.VMEM((192, 128), jnp.float32),
            pltpu.SemaphoreType.DMA((4,)),
            pltpu.SemaphoreType.REGULAR((7,)),
            pltpu.SemaphoreType.DMA((15,)),
            pltpu.SemaphoreType.DMA((15,)),
        ],
        compiler_params=pltpu.CompilerParams(collective_id=0, has_side_effects=True),
        name="chebyshev",
    )(field, links)
    hv, rest = once, twice
    once = hv + cheb_shift * field
    twice = rest - 2.0 * hv
    return once.reshape(vectors.shape), twice.reshape(vectors.shape)


def solution(mesh):
    placed = (P("sa", "gx", "gy", None, None), P("gx", "gy", None, None))
    return jax.shard_map(
        per_device,
        mesh=mesh,
        in_specs=placed,
        out_specs=(placed[0], placed[0]),
        check_vma=False,
    )
```

```python
import functools

import jax
import jax.numpy as jnp
from jax import lax
from jax.experimental import pallas as pl
from jax.experimental.pallas import tpu as pltpu
from jax.sharding import PartitionSpec as P

MESH = pl.DeviceIdType.MESH

m5_height = 1.8
wall_mass = 0.1
cheb_scale = 0.2
cheb_shift = -0.5
diagonal = 5.0 - m5_height
source = ((3, 2), (3, 2), (2, 3), (2, 3))
coefficient = (
    ((0, -1), (0, -1), (0, 1), (0, 1)),
    ((-1, 0), (1, 0), (1, 0), (-1, 0)),
    ((0, -1), (0, 1), (0, 1), (0, -1)),
    ((1, 0), (1, 0), (1, 0), (1, 0)),
)
STRIDE = (2, 1)

GY_UP, GY_DOWN, GX_UP, GX_DOWN, SA_UP, SA_DOWN, MIRROR = range(7)
BACK = (GY_DOWN, GY_UP, GX_DOWN, GX_UP, SA_DOWN, SA_UP, MIRROR)
MAIN, RELAY_UP, RELAY_DOWN = 12, 13, 14


def add_times(base, coef, value):
    re, im = value
    if coef[0] == 1:
        return base[0] + re, base[1] + im
    if coef[0] == -1:
        return base[0] - re, base[1] - im
    if coef[1] == 1:
        return base[0] - im, base[1] + re
    return base[0] + im, base[1] - re


def scaled(coef, sign):
    return coef[0] * sign, coef[1] * sign


def project(field, direction, sign):
    parts = [
        add_times(field(a), scaled(coefficient[direction][a], sign), field(source[direction][a]))
        for a in range(2)
    ]
    return jnp.stack([p[0] for p in parts]), jnp.stack([p[1] for p in parts])


def expand(total, half, direction, sign):
    total = list(total)
    for a in range(2):
        b = source[direction][a]
        value = (half[0][a], half[1][a])
        total[a] = (total[a][0] + value[0], total[a][1] + value[1])
        total[b] = add_times(total[b], scaled(coefficient[direction][b], sign), value)
    return total


def link_of(links, direction):
    base = direction * 18
    re = links[base : base + 9].reshape(3, 3, 8, 128)
    im = links[base + 9 : base + 18].reshape(3, 3, 8, 128)
    return re, im


def link_times(link, half, adjoint):
    re, im = None, None
    for j in range(3):
        u_re = (link[0][j] if adjoint else link[0][:, j])[None]
        u_im = (link[1][j] if adjoint else link[1][:, j])[None]
        h_re, h_im = half[0][:, j][:, None], half[1][:, j][:, None]
        if adjoint:
            t_re = u_re * h_re + u_im * h_im
            t_im = u_re * h_im - u_im * h_re
        else:
            t_re = u_re * h_re - u_im * h_im
            t_im = u_re * h_im + u_im * h_re
        re = t_re if re is None else re + t_re
        im = t_im if im is None else im + t_im
    return re, im


def rolled(value, shift, axis):
    size = value.shape[axis]
    flat = value.reshape((-1,) + value.shape[-2:])
    return pltpu.roll(flat, shift % size, axis + 3).reshape(value.shape)


def masks():
    lane = lax.broadcasted_iota(jnp.int32, (1, 1, 8, 128), 3)
    sub = lax.broadcasted_iota(jnp.int32, (1, 1, 8, 128), 2)
    time = lane % 64
    return {
        "first": time == 0,
        "last": time == 63,
        "zlow": lane < 64,
        "low": tuple((sub // q) % 2 == 0 for q in STRIDE),
    }


def ahead_local(half, direction, mask):
    out = []
    for value in half:
        if direction == 2:
            near = rolled(value, 64, -1)
            out.append(jnp.where(mask["zlow"], near, rolled(near, 4, -2)))
        else:
            out.append(jnp.where(mask["last"], -rolled(value, 63, -1), rolled(value, -1, -1)))
    return out


def behind_local(half, direction, mask):
    out = []
    for value in half:
        if direction == 2:
            near = rolled(value, 64, -1)
            out.append(jnp.where(mask["zlow"], rolled(near, 4, -2), near))
        else:
            out.append(jnp.where(mask["first"], -rolled(value, -63, -1), rolled(value, 1, -1)))
    return out


def kernel(
    v_hbm,
    u_hbm,
    mirrored_ref,
    rest_ref,
    vin,
    uin,
    field_v,
    links,
    field_p,
    field_g,
    field_r,
    face_out,
    face_in,
    chiral_in,
    mirror_in,
    relay_in,
    natural,
    local_sem,
    known_sem,
    send_sem,
    recv_sem,
):
    axes = ("sa", "gx", "gy")
    me = {axis: lax.axis_index(axis) for axis in axes}
    size = {axis: lax.axis_size(axis) for axis in axes}

    def step(axis, by):
        return {axis: lax.rem(me[axis] + by + size[axis], size[axis])}

    target = (
        step("gy", 1),
        step("gy", -1),
        step("gx", 1),
        step("gx", -1),
        step("sa", 1),
        step("sa", -1),
        {"sa": size["sa"] - 1 - me["sa"]},
    )

    def rank(axis, index):
        if axis == "gx":
            return index + 1 - 2 * lax.rem(index, 2)
        if axis == "gy":
            return jnp.where(index < 2, index, 5 - index)
        return index

    first = []
    lowest = me["gy"] == 0
    for way, device in enumerate(target):
        ((axis, index),) = device.items()
        ahead = rank(axis, me[axis]) < rank(axis, index)
        if way in (SA_UP, SA_DOWN):
            wraps = jnp.abs(me[axis] - index) == size[axis] - 1
            ahead = jnp.logical_xor(ahead, jnp.logical_and(lowest, wraps))
        first.append(ahead)
    barrier = pltpu.get_barrier_semaphore()
    for way, device in enumerate(target):

        @pl.when(first[way])
        def _(device=device):
            pl.semaphore_signal(barrier, inc=1, device_id=device, device_id_type=MESH)

    loads = []
    for h in range(2):
        lanes = pl.ds(128 * h, 128)
        loads.append(
            pltpu.make_async_copy(v_hbm.at[:, lanes], vin.at[pl.ds(96 * h, 96)], local_sem.at[h])
        )
        loads.append(
            pltpu.make_async_copy(
                u_hbm.at[:, lanes], uin.at[pl.ds(288 * h, 288)], local_sem.at[2 + h]
            )
        )
    for load in loads:
        load.start()

    copies = {}

    def copy_of(index, way, src, dst):
        copies[index] = pltpu.make_async_remote_copy(
            src_ref=src,
            dst_ref=dst,
            send_sem=send_sem.at[index],
            recv_sem=recv_sem.at[index],
            device_id=target[way],
            device_id_type=MESH,
        )
        return copies[index]

    def meet(way):
        @pl.when(first[way])
        def _():
            pl.semaphore_wait(known_sem.at[way], 1)

    for stage in range(2):
        for way in (GY_UP, GY_DOWN, GX_UP, GX_DOWN):
            slot = stage * 4 + way
            copy_of(stage * 6 + way, way, face_out.at[slot], face_in.at[slot])
    upper, lower = pl.ds(0, 12), pl.ds(12, 12)
    copy_of(SA_UP, SA_UP, field_v.at[upper], chiral_in.at[pl.ds(0, 12)])
    copy_of(SA_DOWN, SA_DOWN, field_v.at[lower], chiral_in.at[pl.ds(12, 12)])
    copy_of(6 + SA_DOWN, SA_DOWN, field_g.at[upper], chiral_in.at[pl.ds(24, 12)])
    copy_of(6 + SA_UP, SA_UP, field_g.at[lower], chiral_in.at[pl.ds(36, 12)])
    copy_of(MAIN, MIRROR, field_p, mirror_in)
    copy_of(RELAY_UP, MIRROR, face_in.at[GY_DOWN], relay_in.at[0])
    copy_of(RELAY_DOWN, MIRROR, face_in.at[GY_UP], relay_in.at[1])

    mask = masks()
    zero = jnp.zeros((3, 8, 128), jnp.float32)
    nothing = [(zero, zero)] * 4

    def reader(ref):
        def spin(a):
            return ref[a * 6 : a * 6 + 3], ref[a * 6 + 3 : a * 6 + 6]

        return spin

    def halves(field, direction, sign):
        ahead = project(field, direction, -sign)
        behind = link_times(link_of(links, direction), project(field, direction, sign), True)
        return ahead, behind

    def pack(pair, direction, stage):
        q = STRIDE[direction]
        low = mask["low"][direction]
        up, down = ((GX_UP, GX_DOWN), (GY_UP, GY_DOWN))[direction]
        ahead, behind = pair
        packed = jnp.where(low, ahead[0], rolled(ahead[1], q, -2))
        face_out[stage * 4 + down] = packed.reshape(6, 8, 128)
        packed = jnp.where(low, rolled(behind[1], -q, -2), behind[0])
        face_out[stage * 4 + up] = packed.reshape(6, 8, 128)

    def unpack(from_up, from_down, direction):
        q = STRIDE[direction]
        from_up = from_up.reshape(2, 3, 8, 128)
        from_down = from_down.reshape(2, 3, 8, 128)
        return (rolled(from_up, q, -2), from_up), (rolled(from_down, -q, -2), from_down)

    def hops_local(total, field, sign):
        for direction in (2, 3):
            link = link_of(links, direction)
            ahead = ahead_local(project(field, direction, -sign), direction, mask)
            total = expand(total, link_times(link, ahead, False), direction, -sign)
            behind = link_times(link, project(field, direction, sign), True)
            total = expand(total, behind_local(behind, direction, mask), direction, sign)
        return total

    def hops_across(total, pair, halo, direction, sign):
        q = STRIDE[direction]
        low = mask["low"][direction]
        ahead, behind = pair
        ahead = [jnp.where(low, rolled(ahead[k], -q, -2), halo[0][k]) for k in range(2)]
        behind = [jnp.where(low, halo[1][k], rolled(behind[k], q, -2)) for k in range(2)]
        link = link_of(links, direction)
        total = expand(total, link_times(link, ahead, False), direction, -sign)
        return expand(total, behind, direction, sign)

    def halo_terms(halo, sign):
        low = mask["low"][1]
        ahead = [jnp.where(low, 0.0, halo[0][k]) for k in range(2)]
        behind = [jnp.where(low, halo[1][k], 0.0) for k in range(2)]
        total = expand(nothing, link_times(link_of(links, 1), ahead, False), 1, -sign)
        return expand(total, behind, 1, sign)

    last = size["sa"] - 1
    from_down = jnp.where(me["sa"] == 0, -wall_mass, 1.0).astype(jnp.float32)
    from_up = jnp.where(me["sa"] == last, -wall_mass, 1.0).astype(jnp.float32)
    no_halo = ((0.0, 0.0), (0.0, 0.0))

    for load in (loads[0], loads[2]):
        load.wait()
    for r in range(24):
        field_v[r] = vin[pl.ds(r, 8, stride=24), :]
    for load in (loads[1], loads[3]):
        load.wait()
    for r in range(18, 36):
        links[r] = uin[pl.ds(r, 8, stride=72), :]

    field = reader(field_v)
    pair_y = halves(field, 1, 1)
    pack(pair_y, 1, 0)
    count = jnp.int32(0)
    for way in range(7):
        count = count + jnp.where(first[way], 0, 1)
    pl.semaphore_wait(barrier, count)
    for way in (GY_UP, GY_DOWN):

        @pl.when(jnp.logical_not(first[way]))
        def _(way=way):
            copies[way].start()

    for way, device in enumerate(target):

        @pl.when(jnp.logical_not(first[way]))
        def _(way=way, device=device):
            pl.semaphore_signal(
                known_sem.at[BACK[way]], inc=1, device_id=device, device_id_type=MESH
            )

    for r in (*range(18), *range(36, 72)):
        links[r] = uin[pl.ds(r, 8, stride=72), :]
    pair_x = halves(field, 0, 1)
    pack(pair_x, 0, 0)
    near = (GX_DOWN, GX_UP, SA_UP, SA_DOWN)
    for way in near:

        @pl.when(jnp.logical_not(first[way]))
        def _(way=way):
            copies[way].start()

    for way in near:

        @pl.when(first[way])
        def _(way=way):
            pl.semaphore_wait(known_sem.at[way], 1)
            copies[way].start()

    total = hops_local(nothing, field, 1)
    total = hops_across(total, pair_y, no_halo, 1, 1)
    copies[GX_DOWN].wait_recv()
    copies[GX_UP].wait_recv()
    halo = unpack(face_in[GX_DOWN], face_in[GX_UP], 0)
    total = hops_across(total, pair_x, halo, 0, 1)
    copies[SA_UP].wait_recv()
    copies[SA_DOWN].wait_recv()
    for a in range(4):
        scale = from_down if a < 2 else from_up
        for part in range(2):
            row = a * 6 + part * 3
            field_p[row : row + 3] = (
                diagonal * field_v[row : row + 3]
                - 0.5 * total[a][part]
                - scale * chiral_in[row : row + 3]
            )
    pack(halves(reader(field_p), 1, -1), 1, 1)
    for way in (GY_UP, GY_DOWN):

        @pl.when(jnp.logical_not(first[way]))
        def _(way=way):
            copies[6 + way].start()

    soon = me["gy"] == 0

    meet(MIRROR)

    @pl.when(soon)
    def _():
        copies[MAIN].start()

    for way, relay in ((GY_UP, RELAY_UP), (GY_DOWN, RELAY_DOWN)):

        @pl.when(first[way])
        def _(way=way):
            pl.semaphore_wait(known_sem.at[way], 1)
            copies[way].start()
            copies[6 + way].start()

        copies[BACK[way]].wait_recv()
        copies[relay].start()

    @pl.when(jnp.logical_not(soon))
    def _():
        copies[MAIN].start()

    halo = unpack(face_in[GY_DOWN], face_in[GY_UP], 1)
    total = halo_terms(halo, 1)
    for a in range(4):
        for part in range(2):
            row = a * 6 + part * 3
            field_g[row : row + 3] = field_p[row : row + 3] - 0.5 * total[a][part]
    copies[6 + SA_DOWN].start()
    copies[6 + SA_UP].start()
    field = reader(field_g)
    pair_x = halves(field, 0, -1)
    pack(pair_x, 0, 1)
    copies[6 + GX_DOWN].start()
    copies[6 + GX_UP].start()
    total = hops_local(nothing, field, -1)
    total = hops_across(total, halves(field, 1, -1), no_halo, 1, -1)
    copies[6 + GX_DOWN].wait_recv()
    copies[6 + GX_UP].wait_recv()
    halo = unpack(face_in[4 + GX_DOWN], face_in[4 + GX_UP], 0)
    total = hops_across(total, pair_x, halo, 0, -1)
    copies[6 + SA_DOWN].wait_recv()
    copies[6 + SA_UP].wait_recv()
    second = 2.0 * cheb_scale * cheb_scale

    def spread(ref):
        for site in range(4):
            for h in range(2):
                block = pl.ds(h * 96 + site * 24, 24)
                ref[pl.ds(site * 24, 24), pl.ds(128 * h, 128)] = natural[block, :]

    for a in range(4):
        scale = from_up if a < 2 else from_down
        for part in range(2):
            row = a * 6 + part * 3
            value = second * (
                diagonal * field_g[row : row + 3]
                - 0.5 * total[a][part]
                - scale * chiral_in[24 + row : 24 + row + 3]
            )
            field_r[row : row + 3] = value + cheb_shift * field_v[row : row + 3]
    for index in (MAIN, RELAY_UP, RELAY_DOWN):
        copies[index].wait_recv()
    total = halo_terms(unpack(relay_in[0], relay_in[1], 1), 1)
    for a in range(4):
        scale = cheb_scale if a < 2 else -cheb_scale
        for part in range(2):
            row = a * 6 + part * 3
            value = scale * (mirror_in[row : row + 3] - 0.5 * total[a][part])
            for c in range(3):
                natural[pl.ds(row + c, 8, stride=24), :] = value[c]
    spread(mirrored_ref)
    copies[6 + GY_DOWN].wait_recv()
    copies[6 + GY_UP].wait_recv()
    halo = unpack(face_in[4 + GY_DOWN], face_in[4 + GY_UP], 1)
    halo = (
        [halo[0][k] - pair_y[1][k] for k in range(2)],
        [halo[1][k] - pair_y[0][k] for k in range(2)],
    )
    late = halo_terms(halo, -1)
    for a in range(4):
        for part in range(2):
            row = a * 6 + part * 3
            value = field_r[row : row + 3] - 0.5 * second * late[a][part]
            for c in range(3):
                natural[pl.ds(row + c, 8, stride=24), :] = value[c]
    spread(rest_ref)
    for copy in copies.values():
        copy.wait_send()


def per_device(vectors, gauge_links):
    field = vectors.reshape(96, 256)
    links = gauge_links.reshape(288, 256)
    shape = pltpu.VMEM((96, 256), jnp.float32)
    once, twice = pl.pallas_call(
        kernel,
        out_shape=(shape, shape),
        in_specs=[pl.BlockSpec(memory_space=pl.ANY)] * 2,
        out_specs=[pl.BlockSpec(memory_space=pltpu.VMEM)] * 2,
        scratch_shapes=[
            pltpu.VMEM((192, 128), jnp.float32),
            pltpu.VMEM((576, 128), jnp.float32),
            pltpu.VMEM((24, 8, 128), jnp.float32),
            pltpu.VMEM((72, 8, 128), jnp.float32),
            pltpu.VMEM((24, 8, 128), jnp.float32),
            pltpu.VMEM((24, 8, 128), jnp.float32),
            pltpu.VMEM((24, 8, 128), jnp.float32),
            pltpu.VMEM((8, 6, 8, 128), jnp.float32),
            pltpu.VMEM((8, 6, 8, 128), jnp.float32),
            pltpu.VMEM((48, 8, 128), jnp.float32),
            pltpu.VMEM((24, 8, 128), jnp.float32),
            pltpu.VMEM((2, 6, 8, 128), jnp.float32),
            pltpu.VMEM((192, 128), jnp.float32),
            pltpu.SemaphoreType.DMA((4,)),
            pltpu.SemaphoreType.REGULAR((7,)),
            pltpu.SemaphoreType.DMA((15,)),
            pltpu.SemaphoreType.DMA((15,)),
        ],
        compiler_params=pltpu.CompilerParams(collective_id=0, has_side_effects=True),
        name="chebyshev",
    )(field, links)
    hv, rest = once, twice
    once = hv + cheb_shift * field
    twice = rest - 2.0 * hv
    return once.reshape(vectors.shape), twice.reshape(vectors.shape)


def solution(mesh):
    placed = (P("sa", "gx", "gy", None, None), P("gx", "gy", None, None))
    return jax.shard_map(
        per_device,
        mesh=mesh,
        in_specs=placed,
        out_specs=(placed[0], placed[0]),
        check_vma=False,
    )
```

```python
import functools

import jax
import jax.numpy as jnp
from jax import lax
from jax.experimental import pallas as pl
from jax.experimental.pallas import tpu as pltpu
from jax.sharding import PartitionSpec as P

MESH = pl.DeviceIdType.MESH

m5_height = 1.8
wall_mass = 0.1
cheb_scale = 0.2
cheb_shift = -0.5
diagonal = 5.0 - m5_height
source = ((3, 2), (3, 2), (2, 3), (2, 3))
coefficient = (
    ((0, -1), (0, -1), (0, 1), (0, 1)),
    ((-1, 0), (1, 0), (1, 0), (-1, 0)),
    ((0, -1), (0, 1), (0, 1), (0, -1)),
    ((1, 0), (1, 0), (1, 0), (1, 0)),
)
STRIDE = (2, 1)

GY_UP, GY_DOWN, GX_UP, GX_DOWN, SA_UP, SA_DOWN, MIRROR = range(7)
BACK = (GY_DOWN, GY_UP, GX_DOWN, GX_UP, SA_DOWN, SA_UP, MIRROR)
MAIN, RELAY_UP, RELAY_DOWN = 12, 13, 14


def add_times(base, coef, value):
    re, im = value
    if coef[0] == 1:
        return base[0] + re, base[1] + im
    if coef[0] == -1:
        return base[0] - re, base[1] - im
    if coef[1] == 1:
        return base[0] - im, base[1] + re
    return base[0] + im, base[1] - re


def scaled(coef, sign):
    return coef[0] * sign, coef[1] * sign


def project(field, direction, sign):
    parts = [
        add_times(field(a), scaled(coefficient[direction][a], sign), field(source[direction][a]))
        for a in range(2)
    ]
    return jnp.stack([p[0] for p in parts]), jnp.stack([p[1] for p in parts])


def expand(total, half, direction, sign):
    total = list(total)
    for a in range(2):
        b = source[direction][a]
        value = (half[0][a], half[1][a])
        total[a] = (total[a][0] + value[0], total[a][1] + value[1])
        total[b] = add_times(total[b], scaled(coefficient[direction][b], sign), value)
    return total


def link_of(links, direction):
    base = direction * 18
    re = links[base : base + 9].reshape(3, 3, 8, 128)
    im = links[base + 9 : base + 18].reshape(3, 3, 8, 128)
    return re, im


def link_times(link, half, adjoint):
    re, im = None, None
    for j in range(3):
        u_re = (link[0][j] if adjoint else link[0][:, j])[None]
        u_im = (link[1][j] if adjoint else link[1][:, j])[None]
        h_re, h_im = half[0][:, j][:, None], half[1][:, j][:, None]
        if adjoint:
            t_re = u_re * h_re + u_im * h_im
            t_im = u_re * h_im - u_im * h_re
        else:
            t_re = u_re * h_re - u_im * h_im
            t_im = u_re * h_im + u_im * h_re
        re = t_re if re is None else re + t_re
        im = t_im if im is None else im + t_im
    return re, im


def rolled(value, shift, axis):
    size = value.shape[axis]
    flat = value.reshape((-1,) + value.shape[-2:])
    return pltpu.roll(flat, shift % size, axis + 3).reshape(value.shape)


def masks():
    lane = lax.broadcasted_iota(jnp.int32, (1, 1, 8, 128), 3)
    sub = lax.broadcasted_iota(jnp.int32, (1, 1, 8, 128), 2)
    time = lane % 64
    return {
        "first": time == 0,
        "last": time == 63,
        "zlow": lane < 64,
        "low": tuple((sub // q) % 2 == 0 for q in STRIDE),
    }


def ahead_local(half, direction, mask):
    out = []
    for value in half:
        if direction == 2:
            near = rolled(value, 64, -1)
            out.append(jnp.where(mask["zlow"], near, rolled(near, 4, -2)))
        else:
            out.append(jnp.where(mask["last"], -rolled(value, 63, -1), rolled(value, -1, -1)))
    return out


def behind_local(half, direction, mask):
    out = []
    for value in half:
        if direction == 2:
            near = rolled(value, 64, -1)
            out.append(jnp.where(mask["zlow"], rolled(near, 4, -2), near))
        else:
            out.append(jnp.where(mask["first"], -rolled(value, -63, -1), rolled(value, 1, -1)))
    return out


def kernel(
    v_hbm,
    u_hbm,
    mirrored_ref,
    rest_ref,
    vin,
    uin,
    field_v,
    links,
    field_p,
    field_g,
    field_r,
    face_out,
    face_in,
    chiral_in,
    mirror_in,
    relay_in,
    natural,
    local_sem,
    known_sem,
    send_sem,
    recv_sem,
):
    axes = ("sa", "gx", "gy")
    me = {axis: lax.axis_index(axis) for axis in axes}
    size = {axis: lax.axis_size(axis) for axis in axes}

    def step(axis, by):
        return {axis: lax.rem(me[axis] + by + size[axis], size[axis])}

    target = (
        step("gy", 1),
        step("gy", -1),
        step("gx", 1),
        step("gx", -1),
        step("sa", 1),
        step("sa", -1),
        {"sa": size["sa"] - 1 - me["sa"]},
    )

    def rank(axis, index):
        if axis == "gy":
            return jnp.where(index < 2, index, 5 - index)
        return index

    first = []
    lowest = me["gy"] == 0
    for way, device in enumerate(target):
        ((axis, index),) = device.items()
        ahead = rank(axis, me[axis]) < rank(axis, index)
        if way in (SA_UP, SA_DOWN):
            wraps = jnp.abs(me[axis] - index) == size[axis] - 1
            ahead = jnp.logical_xor(ahead, jnp.logical_and(lowest, wraps))
        first.append(ahead)
    barrier = pltpu.get_barrier_semaphore()
    for way, device in enumerate(target):

        @pl.when(first[way])
        def _(device=device):
            pl.semaphore_signal(barrier, inc=1, device_id=device, device_id_type=MESH)

    loads = []
    for h in range(2):
        lanes = pl.ds(128 * h, 128)
        loads.append(
            pltpu.make_async_copy(v_hbm.at[:, lanes], vin.at[pl.ds(96 * h, 96)], local_sem.at[h])
        )
        loads.append(
            pltpu.make_async_copy(
                u_hbm.at[:, lanes], uin.at[pl.ds(288 * h, 288)], local_sem.at[2 + h]
            )
        )
    for load in loads:
        load.start()

    copies = {}

    def copy_of(index, way, src, dst):
        copies[index] = pltpu.make_async_remote_copy(
            src_ref=src,
            dst_ref=dst,
            send_sem=send_sem.at[index],
            recv_sem=recv_sem.at[index],
            device_id=target[way],
            device_id_type=MESH,
        )
        return copies[index]

    def meet(way):
        @pl.when(first[way])
        def _():
            pl.semaphore_wait(known_sem.at[way], 1)

    for stage in range(2):
        for way in (GY_UP, GY_DOWN, GX_UP, GX_DOWN):
            slot = stage * 4 + way
            copy_of(stage * 6 + way, way, face_out.at[slot], face_in.at[slot])
    upper, lower = pl.ds(0, 12), pl.ds(12, 12)
    copy_of(SA_UP, SA_UP, field_v.at[upper], chiral_in.at[pl.ds(0, 12)])
    copy_of(SA_DOWN, SA_DOWN, field_v.at[lower], chiral_in.at[pl.ds(12, 12)])
    copy_of(6 + SA_DOWN, SA_DOWN, field_g.at[upper], chiral_in.at[pl.ds(24, 12)])
    copy_of(6 + SA_UP, SA_UP, field_g.at[lower], chiral_in.at[pl.ds(36, 12)])
    copy_of(MAIN, MIRROR, field_p, mirror_in)
    copy_of(RELAY_UP, MIRROR, face_in.at[GY_DOWN], relay_in.at[0])
    copy_of(RELAY_DOWN, MIRROR, face_in.at[GY_UP], relay_in.at[1])

    mask = masks()
    zero = jnp.zeros((3, 8, 128), jnp.float32)
    nothing = [(zero, zero)] * 4

    def reader(ref):
        def spin(a):
            return ref[a * 6 : a * 6 + 3], ref[a * 6 + 3 : a * 6 + 6]

        return spin

    def halves(field, direction, sign):
        ahead = project(field, direction, -sign)
        behind = link_times(link_of(links, direction), project(field, direction, sign), True)
        return ahead, behind

    def pack(pair, direction, stage):
        q = STRIDE[direction]
        low = mask["low"][direction]
        up, down = ((GX_UP, GX_DOWN), (GY_UP, GY_DOWN))[direction]
        ahead, behind = pair
        packed = jnp.where(low, ahead[0], rolled(ahead[1], q, -2))
        face_out[stage * 4 + down] = packed.reshape(6, 8, 128)
        packed = jnp.where(low, rolled(behind[1], -q, -2), behind[0])
        face_out[stage * 4 + up] = packed.reshape(6, 8, 128)

    def unpack(from_up, from_down, direction):
        q = STRIDE[direction]
        from_up = from_up.reshape(2, 3, 8, 128)
        from_down = from_down.reshape(2, 3, 8, 128)
        return (rolled(from_up, q, -2), from_up), (rolled(from_down, -q, -2), from_down)

    def hops_local(total, field, sign):
        for direction in (2, 3):
            link = link_of(links, direction)
            ahead = ahead_local(project(field, direction, -sign), direction, mask)
            total = expand(total, link_times(link, ahead, False), direction, -sign)
            behind = link_times(link, project(field, direction, sign), True)
            total = expand(total, behind_local(behind, direction, mask), direction, sign)
        return total

    def hops_across(total, pair, halo, direction, sign):
        q = STRIDE[direction]
        low = mask["low"][direction]
        ahead, behind = pair
        ahead = [jnp.where(low, rolled(ahead[k], -q, -2), halo[0][k]) for k in range(2)]
        behind = [jnp.where(low, halo[1][k], rolled(behind[k], q, -2)) for k in range(2)]
        link = link_of(links, direction)
        total = expand(total, link_times(link, ahead, False), direction, -sign)
        return expand(total, behind, direction, sign)

    def halo_terms(halo, sign):
        low = mask["low"][1]
        ahead = [jnp.where(low, 0.0, halo[0][k]) for k in range(2)]
        behind = [jnp.where(low, halo[1][k], 0.0) for k in range(2)]
        total = expand(nothing, link_times(link_of(links, 1), ahead, False), 1, -sign)
        return expand(total, behind, 1, sign)

    last = size["sa"] - 1
    from_down = jnp.where(me["sa"] == 0, -wall_mass, 1.0).astype(jnp.float32)
    from_up = jnp.where(me["sa"] == last, -wall_mass, 1.0).astype(jnp.float32)
    no_halo = ((0.0, 0.0), (0.0, 0.0))

    for load in (loads[0], loads[2]):
        load.wait()
    for r in range(24):
        field_v[r] = vin[pl.ds(r, 8, stride=24), :]
    for load in (loads[1], loads[3]):
        load.wait()
    for r in range(18, 36):
        links[r] = uin[pl.ds(r, 8, stride=72), :]

    field = reader(field_v)
    pair_y = halves(field, 1, 1)
    pack(pair_y, 1, 0)
    for r in (*range(18), *range(36, 72)):
        links[r] = uin[pl.ds(r, 8, stride=72), :]
    pair_x = halves(field, 0, 1)
    pack(pair_x, 0, 0)
    count = jnp.int32(0)
    for way in range(7):
        count = count + jnp.where(first[way], 0, 1)
    pl.semaphore_wait(barrier, count)
    for way in (GY_UP, GY_DOWN):

        @pl.when(jnp.logical_not(first[way]))
        def _(way=way):
            copies[way].start()

    for way, device in enumerate(target):

        @pl.when(jnp.logical_not(first[way]))
        def _(way=way, device=device):
            pl.semaphore_signal(
                known_sem.at[BACK[way]], inc=1, device_id=device, device_id_type=MESH
            )

    near = (GX_DOWN, GX_UP, SA_UP, SA_DOWN)
    for way in near:

        @pl.when(jnp.logical_not(first[way]))
        def _(way=way):
            copies[way].start()

    for way in near:

        @pl.when(first[way])
        def _(way=way):
            pl.semaphore_wait(known_sem.at[way], 1)
            copies[way].start()

    total = hops_local(nothing, field, 1)
    total = hops_across(total, pair_y, no_halo, 1, 1)
    copies[GX_DOWN].wait_recv()
    copies[GX_UP].wait_recv()
    halo = unpack(face_in[GX_DOWN], face_in[GX_UP], 0)
    total = hops_across(total, pair_x, halo, 0, 1)
    copies[SA_UP].wait_recv()
    copies[SA_DOWN].wait_recv()
    for a in range(4):
        scale = from_down if a < 2 else from_up
        for part in range(2):
            row = a * 6 + part * 3
            field_p[row : row + 3] = (
                diagonal * field_v[row : row + 3]
                - 0.5 * total[a][part]
                - scale * chiral_in[row : row + 3]
            )
    pack(halves(reader(field_p), 1, -1), 1, 1)
    for way in (GY_UP, GY_DOWN):

        @pl.when(jnp.logical_not(first[way]))
        def _(way=way):
            copies[6 + way].start()

    soon = me["gy"] == 0

    meet(MIRROR)

    @pl.when(soon)
    def _():
        copies[MAIN].start()

    for way, relay in ((GY_UP, RELAY_UP), (GY_DOWN, RELAY_DOWN)):

        @pl.when(first[way])
        def _(way=way):
            pl.semaphore_wait(known_sem.at[way], 1)
            copies[way].start()
            copies[6 + way].start()

        copies[BACK[way]].wait_recv()
        copies[relay].start()

    @pl.when(jnp.logical_not(soon))
    def _():
        copies[MAIN].start()

    halo = unpack(face_in[GY_DOWN], face_in[GY_UP], 1)
    total = halo_terms(halo, 1)
    for a in range(4):
        for part in range(2):
            row = a * 6 + part * 3
            field_g[row : row + 3] = field_p[row : row + 3] - 0.5 * total[a][part]
    copies[6 + SA_DOWN].start()
    copies[6 + SA_UP].start()
    field = reader(field_g)
    pair_x = halves(field, 0, -1)
    pack(pair_x, 0, 1)
    copies[6 + GX_DOWN].start()
    copies[6 + GX_UP].start()
    total = hops_local(nothing, field, -1)
    total = hops_across(total, halves(field, 1, -1), no_halo, 1, -1)
    copies[6 + GX_DOWN].wait_recv()
    copies[6 + GX_UP].wait_recv()
    halo = unpack(face_in[4 + GX_DOWN], face_in[4 + GX_UP], 0)
    total = hops_across(total, pair_x, halo, 0, -1)
    copies[6 + SA_DOWN].wait_recv()
    copies[6 + SA_UP].wait_recv()
    second = 2.0 * cheb_scale * cheb_scale

    def spread(ref):
        for site in range(4):
            for h in range(2):
                block = pl.ds(h * 96 + site * 24, 24)
                ref[pl.ds(site * 24, 24), pl.ds(128 * h, 128)] = natural[block, :]

    for a in range(4):
        scale = from_up if a < 2 else from_down
        for part in range(2):
            row = a * 6 + part * 3
            value = second * (
                diagonal * field_g[row : row + 3]
                - 0.5 * total[a][part]
                - scale * chiral_in[24 + row : 24 + row + 3]
            )
            field_r[row : row + 3] = value + cheb_shift * field_v[row : row + 3]
    for index in (MAIN, RELAY_UP, RELAY_DOWN):
        copies[index].wait_recv()
    total = halo_terms(unpack(relay_in[0], relay_in[1], 1), 1)
    for a in range(4):
        scale = cheb_scale if a < 2 else -cheb_scale
        for part in range(2):
            row = a * 6 + part * 3
            value = scale * (mirror_in[row : row + 3] - 0.5 * total[a][part])
            for c in range(3):
                natural[pl.ds(row + c, 8, stride=24), :] = value[c]
    spread(mirrored_ref)
    copies[6 + GY_DOWN].wait_recv()
    copies[6 + GY_UP].wait_recv()
    halo = unpack(face_in[4 + GY_DOWN], face_in[4 + GY_UP], 1)
    halo = (
        [halo[0][k] - pair_y[1][k] for k in range(2)],
        [halo[1][k] - pair_y[0][k] for k in range(2)],
    )
    late = halo_terms(halo, -1)
    for a in range(4):
        for part in range(2):
            row = a * 6 + part * 3
            value = field_r[row : row + 3] - 0.5 * second * late[a][part]
            for c in range(3):
                natural[pl.ds(row + c, 8, stride=24), :] = value[c]
    spread(rest_ref)
    for copy in copies.values():
        copy.wait_send()


def per_device(vectors, gauge_links):
    field = vectors.reshape(96, 256)
    links = gauge_links.reshape(288, 256)
    shape = pltpu.VMEM((96, 256), jnp.float32)
    once, twice = pl.pallas_call(
        kernel,
        out_shape=(shape, shape),
        in_specs=[pl.BlockSpec(memory_space=pl.ANY)] * 2,
        out_specs=[pl.BlockSpec(memory_space=pltpu.VMEM)] * 2,
        scratch_shapes=[
            pltpu.VMEM((192, 128), jnp.float32),
            pltpu.VMEM((576, 128), jnp.float32),
            pltpu.VMEM((24, 8, 128), jnp.float32),
            pltpu.VMEM((72, 8, 128), jnp.float32),
            pltpu.VMEM((24, 8, 128), jnp.float32),
            pltpu.VMEM((24, 8, 128), jnp.float32),
            pltpu.VMEM((24, 8, 128), jnp.float32),
            pltpu.VMEM((8, 6, 8, 128), jnp.float32),
            pltpu.VMEM((8, 6, 8, 128), jnp.float32),
            pltpu.VMEM((48, 8, 128), jnp.float32),
            pltpu.VMEM((24, 8, 128), jnp.float32),
            pltpu.VMEM((2, 6, 8, 128), jnp.float32),
            pltpu.VMEM((192, 128), jnp.float32),
            pltpu.SemaphoreType.DMA((4,)),
            pltpu.SemaphoreType.REGULAR((7,)),
            pltpu.SemaphoreType.DMA((15,)),
            pltpu.SemaphoreType.DMA((15,)),
        ],
        compiler_params=pltpu.CompilerParams(collective_id=0, has_side_effects=True),
        name="chebyshev",
    )(field, links)
    hv, rest = once, twice
    once = hv + cheb_shift * field
    twice = rest - 2.0 * hv
    return once.reshape(vectors.shape), twice.reshape(vectors.shape)


def solution(mesh):
    placed = (P("sa", "gx", "gy", None, None), P("gx", "gy", None, None))
    return jax.shard_map(
        per_device,
        mesh=mesh,
        in_specs=placed,
        out_specs=(placed[0], placed[0]),
        check_vma=False,
    )
```
